256 devices in a mesh: cp: 32 (over y_hi, z, core), vocab: 8 (over y_lo, x).
Axes of the slice: x: 4, y: 4 (y_hi: 2, y_lo: 2; y = y_hi * 2 + y_lo), z: 8, core: 2. Of those that a mesh axis runs over, the one named last changes fastest.
Arguments:
- queries: bfloat16 [4096, 4096], P('cp', 'vocab'), may hold values from -160 to 160
- key_states: bfloat16 [4096, 1024], P('cp', 'vocab'), may hold values from -6 to 6
- value_states: bfloat16 [4096, 1024], P('cp', 'vocab'), may hold values from -6 to 6
- out_grad: bfloat16 [4096, 4096], P('cp', 'vocab'), may hold values from -6 to 6
- o_weight: bfloat16 [4096, 4096], P('vocab'), may hold values from -0.09375 to 0.09375
- span_order: int32 [64], replicated, may hold values from 0 to 63, each once
Outputs:
- query_grad: float32 [4096, 4096], P('cp', 'vocab')
- key_grad: float32 [4096, 1024], P('cp', 'vocab')
- value_grad: float32 [4096, 1024], P('cp', 'vocab')
The draws below stay inside these ranges and needn't reach their ends.
Inputs may be any that keep to these rules, and one draw needn't show every extreme that they name: `span_order`: each of the 64 span indices once.
All inputs are finite; a program needn't handle non-finite values.
Results may differ from the reference program's by a relative error of at most 0.014.
Values may be sent and summed in bfloat16 or wider, within the bound.
No kernel may reach another device: no remote copies, remote signals or barrier semaphores. Data moves between devices by JAX's collectives and lax.ppermute only.
A program may use at most 64 MiB of HBM per device.

```python
import jax
import jax.numpy as jnp
from jax import lax

D = 4096
HEADS = 32
KV_HEADS = 8
HEAD_DIM = 128
TOK_DEV = 128
SEQ = 4096
SPANS = 64


def attention_pair(key):
    base_key = jax.random.fold_in(key, 7101)
    split_keys = jax.random.split(base_key, 2)
    key_values = jnp.clip(jax.random.normal(split_keys[0], (SEQ, KV_HEADS, 1, HEAD_DIM), jnp.float32), -6.0, 6.0)
    query_values = jnp.clip(jax.random.normal(split_keys[1], (SEQ, KV_HEADS, HEADS // KV_HEADS, HEAD_DIM), jnp.float32), -6.0, 6.0)
    return (query_values.reshape(SEQ, HEADS * HEAD_DIM), key_values.reshape(SEQ, KV_HEADS * HEAD_DIM))


def draw_queries(key, part):
    return attention_pair(key)[0].astype(jnp.bfloat16)


def draw_key_states(key, part):
    return attention_pair(key)[1].astype(jnp.bfloat16)


def level_of(own_key, dims, shards, low, largest):
    def one(axis_at, parts):
        steps = jax.random.uniform(jax.random.fold_in(jax.random.fold_in(own_key, 6), axis_at), (parts,), jnp.float32, low / len(shards), largest / len(shards))
        return jnp.repeat(jnp.exp(steps), dims[axis_at] // parts).reshape((-1,) + (1,) * (len(dims) - axis_at - 1))

    gain = one(*shards[0])
    for cut in shards[1:]:
        gain = gain * one(*cut)
    return gain


def bell_draw(rng, dims, scale, limit, pieces=(), held_as=jnp.bfloat16):
    drawn = jax.random.normal(rng, dims, jnp.float32) * scale
    if len(pieces) > 0:
        drawn = level_of(rng, dims, pieces, -0.22, 0.18) * drawn
    return jnp.clip(drawn, min=-limit, max=limit).astype(held_as)


def setup_inputs(seed: int = 0) -> dict:
    key_of = jax.random.split(jax.random.key(seed), 7)
    return {
        "queries": draw_queries(jax.random.fold_in(key_of[6], 71), 0),
        "key_states": draw_key_states(jax.random.fold_in(key_of[6], 71), 0),
        "value_states": bell_draw(key_of[2], (SEQ, KV_HEADS * HEAD_DIM), 1.0, 6.0, ((0, 32), (1, 8))),
        "out_grad": bell_draw(key_of[3], (SEQ, D), 1.0, 6.0, ((0, 32), (1, 8))),
        "o_weight": bell_draw(key_of[4], (HEADS * HEAD_DIM, D), D ** -0.5, 0.09375, ((0, 8),)),
        "span_order": jax.random.permutation(key_of[5], SPANS).astype(jnp.int32),
    }


def positions(span_order, span_rows):
    offsets = jnp.arange(span_rows, dtype=jnp.int32)
    return (span_order.astype(jnp.int32)[:, None] * span_rows + offsets[None, :]).reshape(-1)


def attention_grads(queries, key_states, value_states, upstream, places):
    seq_len = queries.shape[0]
    groups = HEADS // KV_HEADS
    factor = HEAD_DIM ** -0.5
    block_rows = TOK_DEV * 8
    block_count = seq_len // block_rows
    query_heads = queries.reshape(seq_len, KV_HEADS, groups, HEAD_DIM).transpose(1, 2, 0, 3).astype(jnp.float32)
    upstream_heads = upstream.reshape(seq_len, KV_HEADS, groups, HEAD_DIM).transpose(1, 2, 0, 3).astype(jnp.float32)
    key_heads = key_states.reshape(seq_len, KV_HEADS, HEAD_DIM).transpose(1, 0, 2).astype(jnp.float32)
    value_heads = value_states.reshape(seq_len, KV_HEADS, HEAD_DIM).transpose(1, 0, 2).astype(jnp.float32)

    def one_head(operands):
        head_queries, head_upstream, head_keys, head_values = operands

        def block_step(carried, block_index):
            key_total, value_total = carried
            offset = block_index * block_rows
            rows_query = lax.dynamic_slice_in_dim(head_queries, offset, block_rows, 1)
            rows_upstream = lax.dynamic_slice_in_dim(head_upstream, offset, block_rows, 1)
            query_places = lax.dynamic_slice_in_dim(places, offset, block_rows, 0)
            visible = places[None, :] <= query_places[:, None]
            scores = jnp.einsum("gqd,sd->gqs", rows_query, head_keys) * factor
            scores = jnp.where(visible[None], scores, -jnp.inf)
            row_peak = jnp.max(scores, axis=2, keepdims=True)
            logsum = row_peak + jnp.log(jnp.sum(jnp.exp(scores - row_peak), axis=2, keepdims=True))
            weights = jnp.exp(scores - logsum)
            grad_probs = jnp.einsum("gqd,sd->gqs", rows_upstream, head_values)
            deltas = jnp.sum(weights * grad_probs, axis=2, keepdims=True)
            grad_scores = lax.optimization_barrier((weights * (grad_probs - deltas)).astype(jnp.bfloat16)).astype(jnp.float32)
            weights_low = lax.optimization_barrier(weights.astype(jnp.bfloat16)).astype(jnp.float32)
            query_block = jnp.einsum("gqs,sd->gqd", grad_scores, head_keys) * factor
            key_total = key_total + jnp.einsum("gqs,gqd->sd", grad_scores, rows_query) * factor
            value_total = value_total + jnp.einsum("gqs,gqd->sd", weights_low, rows_upstream)
            return (key_total, value_total), query_block

        zeros = jnp.zeros((seq_len, HEAD_DIM), jnp.float32)
        (key_total, value_total), query_stack = lax.scan(block_step, (zeros, zeros), jnp.arange(block_count, dtype=jnp.int32))
        query_total = query_stack.transpose(1, 0, 2, 3).reshape(groups, seq_len, HEAD_DIM)
        return key_total, value_total, query_total

    key_grads, value_grads, query_grads = lax.map(one_head, (query_heads, upstream_heads, key_heads, value_heads))
    query_grad = query_grads.transpose(2, 0, 1, 3).reshape(seq_len, HEADS * HEAD_DIM)
    key_grad = key_grads.transpose(1, 0, 2).reshape(seq_len, KV_HEADS * HEAD_DIM)
    value_grad = value_grads.transpose(1, 0, 2).reshape(seq_len, KV_HEADS * HEAD_DIM)
    return query_grad, key_grad, value_grad


def reference(queries, key_states, value_states, out_grad, o_weight, span_order):
    upstream = lax.dot_general(out_grad, o_weight, (((1,), (1,)), ((), ())), preferred_element_type=jnp.float32).astype(jnp.bfloat16)
    places = positions(span_order, TOK_DEV // 2)
    query_grad, key_grad, value_grad = attention_grads(queries, key_states, value_states, upstream, places)
    return query_grad, key_grad, value_grad
```

```python
import math

import jax
import jax.numpy as jnp
from jax import lax
from jax.experimental import pallas as pl
from jax.experimental.pallas import tpu as pltpu
from jax.sharding import Mesh
from jax.sharding import PartitionSpec as P

HEADS = 32
KV_HEADS = 8
HEAD_DIM = 128
GROUPS = HEADS // KV_HEADS
SPAN = 64
CP = ("yh", "z", "c")
VOCAB = ("yl", "x")
FACTOR = HEAD_DIM**-0.5
SCALE2 = FACTOR * math.log2(math.e)
MASKED = -1e30
CHUNK = 256
VMEM_LIMIT = 48 * 1024 * 1024
NT = (((1,), (1,)), ((), ()))
NN = (((1,), (0,)), ((), ()))


def mm(a, b, dims):
    return lax.dot_general(a, b, dims, preferred_element_type=jnp.float32)


def shift_by(value, axes, steps):
    sizes = [lax.axis_size(a) for a in axes]
    total = math.prod(sizes)
    pairs = []
    for src in range(total):
        rest, at = src, []
        for n in reversed(sizes):
            at.insert(0, rest % n)
            rest //= n
        dst = 0
        for n, i, s in zip(sizes, at, steps):
            dst = dst * n + (i + s) % n
        pairs.append((src, dst))
    return lax.ppermute(value, axes, pairs)


def joined(refs):
    return jnp.concatenate([r[...] for r in refs], axis=0)


def fill_bias(kpos_ref, qpos_ref, bias_ref):
    @pl.when(pl.program_id(0) == 0)
    def _():
        for at in range(0, bias_ref.shape[0], CHUNK):
            rows = pl.ds(at, CHUNK)
            visible = kpos_ref[rows, :] <= qpos_ref[...]
            bias_ref[rows, :] = jnp.where(visible, 0.0, MASKED)


def stats_kernel(kpos, qpos, q0, q1, q2, q3, k, lse_ref, bias, s_scr):
    fill_bias(kpos, qpos, bias)
    q = joined((q0, q1, q2, q3))
    keys = k.shape[0]
    peak = jnp.full((1, q.shape[0]), MASKED, jnp.float32)
    for at in range(0, keys, CHUNK):
        rows = pl.ds(at, CHUNK)
        s = mm(k[rows, :], q, NT) * SCALE2 + bias[rows, :]
        s_scr[rows, :] = s
        peak = jnp.maximum(peak, jnp.max(s, axis=0, keepdims=True))
    total = jnp.zeros_like(peak)
    for at in range(0, keys, CHUNK):
        total = total + jnp.sum(jnp.exp2(s_scr[pl.ds(at, CHUNK), :] - peak), axis=0, keepdims=True)
    lse_ref[0] = peak + jnp.log2(total)


def aligned(own, far, core, both):
    n = own.shape[1] // 4

    def pick(a, order):
        return jnp.concatenate([a[:, g * n : (g + 1) * n] for g in order], axis=1)

    return own, pick(far, (1, 0, 3, 2)), pick(core, (2, 3, 0, 1)), pick(both, (3, 2, 1, 0))


def delta_kernel(
    kpos, qpos, q0, q1, q2, q3, u0, u1, u2, u3, k, v, l0, l1, l2, l3, lse_ref, delta_ref, bias
):
    fill_bias(kpos, qpos, bias)
    q, u = joined((q0, q1, q2, q3)), joined((u0, u1, u2, u3))
    parts = aligned(l0[0], l1[0], l2[0], l3[0])
    peak = jnp.maximum(jnp.maximum(parts[0], parts[1]), jnp.maximum(parts[2], parts[3]))
    lse = peak + jnp.log2(sum(jnp.exp2(p - peak) for p in parts))
    lse_ref[0] = lse
    total = jnp.zeros_like(lse)
    for at in range(0, k.shape[0], CHUNK):
        rows = pl.ds(at, CHUNK)
        w = jnp.exp2(mm(k[rows, :], q, NT) * SCALE2 + bias[rows, :] - lse)
        total = total + jnp.sum(w * mm(v[rows, :], u, NT), axis=0, keepdims=True)
    delta_ref[0] = total


def grad_kernel(
    kpos, qpos, q0, q1, q2, q3, u0, u1, u2, u3, k, v, kt, lse_in, d0, d1, d2, d3,
    own_ref, far_ref, core_ref, both_ref, terms_ref, bias, dk, dv,
):
    fill_bias(kpos, qpos, bias)
    head = pl.program_id(0)
    q, u = joined((q0, q1, q2, q3)), joined((u0, u1, u2, u3))
    lse = lse_in[0]
    delta = sum(aligned(d0[0], d1[0], d2[0], d3[0]))

    @pl.when(head == 0)
    def _():
        dk[...] = jnp.zeros_like(dk)
        dv[...] = jnp.zeros_like(dv)

    dq = jnp.zeros((HEAD_DIM, q.shape[0]), jnp.float32)
    for at in range(0, k.shape[0], CHUNK):
        rows = pl.ds(at, CHUNK)
        w = jnp.exp2(mm(k[rows, :], q, NT) * SCALE2 + bias[rows, :] - lse)
        ds = (w * (mm(v[rows, :], u, NT) - delta)).astype(jnp.bfloat16)
        dv[rows, :] += mm(w.astype(jnp.bfloat16), u, NN)
        dk[rows, :] += mm(ds, q, NN)
        dq = dq + mm(kt[:, at : at + CHUNK], ds, NN)
    dq = (dq * FACTOR).T
    n = own_ref.shape[0]
    own_ref[...] = dq[:n]
    far_ref[...] = dq[n : 2 * n]
    core_ref[...] = dq[2 * n : 3 * n].astype(jnp.bfloat16)
    both_ref[...] = dq[3 * n :].astype(jnp.bfloat16)

    @pl.when(head == pl.num_programs(0) - 1)
    def _():
        terms_ref[:, :HEAD_DIM] = (dk[...] * FACTOR).astype(jnp.bfloat16)
        terms_ref[:, HEAD_DIM:] = dv[...].astype(jnp.bfloat16)


def upstream_kernel(order, *refs):
    parts, w, out, acc = refs[:-3], refs[-3], refs[-2], refs[-1]
    step = pl.program_id(0)
    for i, part in enumerate(parts):

        @pl.when(step == i)
        def _(i=i, part=part):
            term = mm(part[...], w[...], NT)
            if i == 0:
                acc[...] = term
            elif i == len(parts) - 1:
                out[...] = (acc[...] + term).astype(out.dtype)
            else:
                acc[...] += term


def whole(shape):
    return pl.BlockSpec(shape, lambda h: (0,) * len(shape))


def upstream_of(parts, order, o_weight):
    rows, width = parts[0].shape
    cols = o_weight.shape[0]

    def const(shape):
        return pl.BlockSpec(shape, lambda i, o: (0, 0))

    return pl.pallas_call(
        upstream_kernel,
        out_shape=jax.ShapeDtypeStruct((rows, cols), jnp.bfloat16),
        grid_spec=pltpu.PrefetchScalarGridSpec(
            num_scalar_prefetch=1,
            grid=(len(parts),),
            in_specs=[const((rows, width))] * len(parts)
            + [pl.BlockSpec((cols, width), lambda i, o: (0, o[i]))],
            out_specs=const((rows, cols)),
            scratch_shapes=[pltpu.VMEM((rows, cols), jnp.float32)],
        ),
        compiler_params=pltpu.CompilerParams(vmem_limit_bytes=VMEM_LIMIT),
        name="upstream",
    )(order, *parts, o_weight)


def local(queries, key_states, value_states, out_grad, o_weight, span_order):
    rows = queries.shape[0]
    nz = lax.axis_size("z")
    nx = lax.axis_size("x")
    keys = nz * rows
    many = 4 * rows
    f32, bf16 = jnp.float32, jnp.bfloat16
    yh, z, c = lax.axis_index("yh"), lax.axis_index("z"), lax.axis_index("c")
    yl, x = lax.axis_index("yl"), lax.axis_index("x")

    both = jnp.concatenate((key_states, value_states), axis=1)
    kv = lax.all_to_all(
        jnp.broadcast_to(both[None], (nz, *both.shape)), "z", 0, 0, tiled=True
    ).reshape(keys, 2 * HEAD_DIM)
    k_all, v_all = kv[:, :HEAD_DIM], kv[:, HEAD_DIM:]
    kt_all = k_all.T

    parts, sources = [out_grad], [yl * nx + x]
    for steps in ((0, 1), (0, 3), (1, 0), (0, 2), (1, 1), (1, 3), (1, 2)):
        parts.append(shift_by(out_grad, VOCAB, steps))
        sources.append((yl - steps[0]) % 2 * nx + (x - steps[1]) % nx)
    order = jnp.stack(sources).astype(jnp.int32)

    def shared(own):
        far = shift_by(own, ("yh",), (1,))
        return own, far, shift_by(own, ("c",), (1,)), shift_by(far, ("c",), (1,))

    def everyone(own):
        return (
            own,
            shift_by(own, ("yh",), (1,)),
            shift_by(own, ("c",), (1,)),
            shift_by(own, ("yh", "c"), (1, 1)),
        )

    spans = span_order.reshape(2, nz, 2, 2)
    offsets = jnp.arange(SPAN, dtype=jnp.int32)
    key_spans = lax.dynamic_slice(spans, (yh, 0, c, 0), (1, nz, 1, 2)).reshape(2 * nz, 1)
    kpos = (key_spans * SPAN + offsets[None, :]).reshape(keys, 1)
    groups = [(yh, c), (1 - yh, c), (yh, 1 - c), (1 - yh, 1 - c)]
    query_spans = jnp.concatenate(
        [lax.dynamic_slice(spans, (a, z, b, 0), (1, 1, 1, 2)).reshape(2, 1) for a, b in groups]
    )
    qpos = (query_spans * SPAN + offsets[None, :]).reshape(1, many)

    head_block = pl.BlockSpec((rows, HEAD_DIM), lambda h: (0, h))
    row_block = pl.BlockSpec((1, 1, many), lambda h: (h, 0, 0))
    row_shape = jax.ShapeDtypeStruct((GROUPS, 1, many), f32)
    places = [whole((keys, 1)), whole((1, many))]
    key_block = whole((keys, HEAD_DIM))
    bias = pltpu.VMEM((keys, many), f32)
    params = pltpu.CompilerParams(vmem_limit_bytes=VMEM_LIMIT)

    q = shared(queries)
    lse = pl.pallas_call(
        stats_kernel,
        grid=(GROUPS,),
        out_shape=row_shape,
        in_specs=places + [head_block] * 4 + [key_block],
        out_specs=row_block,
        scratch_shapes=[bias, bias],
        compiler_params=params,
        name="row_stats",
    )(kpos, qpos, *q, k_all)
    lse_parts = everyone(lse)

    upstream = upstream_of(parts, order, o_weight)
    u = shared(upstream)
    lse_all, delta = pl.pallas_call(
        delta_kernel,
        grid=(GROUPS,),
        out_shape=(row_shape, row_shape),
        in_specs=places + [head_block] * 8 + [key_block] * 2 + [row_block] * 4,
        out_specs=(row_block, row_block),
        scratch_shapes=[bias],
        compiler_params=params,
        name="row_delta",
    )(kpos, qpos, *q, *u, k_all, v_all, *lse_parts)
    delta_parts = everyone(delta)

    wide = (rows, GROUPS * HEAD_DIM)
    own, far, core, across, terms = pl.pallas_call(
        grad_kernel,
        grid=(GROUPS,),
        out_shape=(
            jax.ShapeDtypeStruct(wide, f32),
            jax.ShapeDtypeStruct(wide, f32),
            jax.ShapeDtypeStruct(wide, bf16),
            jax.ShapeDtypeStruct(wide, bf16),
            jax.ShapeDtypeStruct((keys, 2 * HEAD_DIM), bf16),
        ),
        in_specs=places
        + [head_block] * 8
        + [key_block] * 2
        + [whole((HEAD_DIM, keys))]
        + [row_block] * 5,
        out_specs=(head_block,) * 4 + (whole((keys, 2 * HEAD_DIM)),),
        scratch_shapes=[bias, pltpu.VMEM((keys, HEAD_DIM), f32), pltpu.VMEM((keys, HEAD_DIM), f32)],
        compiler_params=params,
        name="gradients",
    )(kpos, qpos, *q, *u, k_all, v_all, kt_all, lse_all, *delta_parts)

    summed = lax.all_to_all(terms.reshape(nz, rows, 2 * HEAD_DIM), "z", 0, 0, tiled=True)
    summed = jnp.sum(summed.astype(f32), axis=0)
    own = own + shift_by(core, ("c",), (1,)).astype(f32)
    far = far + shift_by(across, ("c",), (1,)).astype(f32)
    query_grad = own + shift_by(far.astype(bf16), ("yh",), (1,)).astype(f32)
    return query_grad, summed[:, :HEAD_DIM], summed[:, HEAD_DIM:]


def solution(mesh):
    finer = Mesh(mesh.devices.reshape(2, 8, 2, 2, 4), CP + VOCAB)
    return jax.shard_map(
        local,
        mesh=finer,
        in_specs=(P(CP, VOCAB), P(CP, VOCAB), P(CP, VOCAB), P(CP, VOCAB), P(VOCAB, None), P()),
        out_specs=(P(CP, VOCAB), P(CP, VOCAB), P(CP, VOCAB)),
        check_vma=False,
    )
```

```python
import math

import jax
import jax.numpy as jnp
from jax import lax
from jax.experimental import pallas as pl
from jax.experimental.pallas import tpu as pltpu
from jax.sharding import Mesh
from jax.sharding import PartitionSpec as P

HEADS = 32
KV_HEADS = 8
HEAD_DIM = 128
GROUPS = HEADS // KV_HEADS
SPAN = 64
CP = ("yh", "z", "c")
VOCAB = ("yl", "x")
FACTOR = HEAD_DIM**-0.5
SCALE2 = FACTOR * math.log2(math.e)
MASKED = -1e30
CHUNK = 256
EXTRA = 16
VMEM_LIMIT = 32 * 1024 * 1024
NT = (((1,), (1,)), ((), ()))
NN = (((1,), (0,)), ((), ()))


def mm(a, b, dims):
    return lax.dot_general(a, b, dims, preferred_element_type=jnp.float32)


def shift_by(value, axes, steps):
    sizes = [lax.axis_size(a) for a in axes]
    total = math.prod(sizes)
    pairs = []
    for src in range(total):
        rest, at = src, []
        for n in reversed(sizes):
            at.insert(0, rest % n)
            rest //= n
        dst = 0
        for n, i, s in zip(sizes, at, steps):
            dst = dst * n + (i + s) % n
        pairs.append((src, dst))
    return lax.ppermute(value, axes, pairs)


def joined(refs):
    return jnp.concatenate([r[...] for r in refs], axis=0)


def fill_bias(kpos_ref, qpos_ref, bias_ref):
    @pl.when(pl.program_id(0) == 0)
    def _():
        for at in range(0, bias_ref.shape[0], CHUNK):
            rows = pl.ds(at, CHUNK)
            visible = kpos_ref[rows, :] <= qpos_ref[...]
            bias_ref[rows, :] = jnp.where(visible, 0.0, MASKED)


def stats_kernel(kpos, qpos, q0, q1, q2, q3, k, lse_ref, bias, s_scr):
    fill_bias(kpos, qpos, bias)
    q = joined((q0, q1, q2, q3))
    keys = k.shape[0]
    peak = jnp.full((1, q.shape[0]), MASKED, jnp.float32)
    for at in range(0, keys, CHUNK):
        rows = pl.ds(at, CHUNK)
        s = mm(k[rows, :], q, NT) * SCALE2 + bias[rows, :]
        s_scr[rows, :] = s
        peak = jnp.maximum(peak, jnp.max(s, axis=0, keepdims=True))
    total = jnp.zeros_like(peak)
    for at in range(0, keys, CHUNK):
        total = total + jnp.sum(jnp.exp2(s_scr[pl.ds(at, CHUNK), :] - peak), axis=0, keepdims=True)
    lse_ref[0] = peak + jnp.log2(total)


def aligned(own, far, core, both):
    n = own.shape[1] // 4

    def pick(a, order):
        return jnp.concatenate([a[:, g * n : (g + 1) * n] for g in order], axis=1)

    return own, pick(far, (1, 0, 3, 2)), pick(core, (2, 3, 0, 1)), pick(both, (3, 2, 1, 0))


def whole_row(ref, head):
    at = 3 * head
    parts = ref[...].astype(jnp.float32)
    row = lax.broadcasted_iota(jnp.int32, parts.shape, 0)
    return jnp.sum(jnp.where((row >= at) & (row < at + 3), parts, 0.0), axis=0, keepdims=True)


def delta_kernel(
    kpos, qpos, q0, q1, q2, q3, u0, u1, u2, u3, k, v, l0, l1, l2, l3, lse_ref, delta_ref, bias
):
    fill_bias(kpos, qpos, bias)
    q, u = joined((q0, q1, q2, q3)), joined((u0, u1, u2, u3))
    parts = aligned(*(whole_row(r, pl.program_id(0)) for r in (l0, l1, l2, l3)))
    peak = jnp.maximum(jnp.maximum(parts[0], parts[1]), jnp.maximum(parts[2], parts[3]))
    lse = peak + jnp.log2(sum(jnp.exp2(p - peak) for p in parts))
    lse_ref[0] = lse
    total = jnp.zeros_like(lse)
    for at in range(0, k.shape[0], CHUNK):
        rows = pl.ds(at, CHUNK)
        w = jnp.exp2(mm(k[rows, :], q, NT) * SCALE2 + bias[rows, :] - lse)
        total = total + jnp.sum(w * mm(v[rows, :], u, NT), axis=0, keepdims=True)
    delta_ref[0] = total


def grad_kernel(
    kpos, qpos, q0, q1, q2, q3, u0, u1, u2, u3, k, v, lse_in, d0, d1, d2, d3,
    own_ref, far_ref, core_ref, both_ref, terms_ref, bias, dk, dv, kt,
):
    fill_bias(kpos, qpos, bias)
    head = pl.program_id(0)
    q, u = joined((q0, q1, q2, q3)), joined((u0, u1, u2, u3))
    lse = lse_in[0]
    delta = sum(aligned(d0[0], d1[0], d2[0], d3[0]))

    @pl.when(head == 0)
    def _():
        dk[...] = jnp.zeros_like(dk)
        dv[...] = jnp.zeros_like(dv)
        kt[...] = k[...].T

    dq = jnp.zeros((HEAD_DIM, q.shape[0]), jnp.float32)
    for at in range(0, k.shape[0], CHUNK):
        rows = pl.ds(at, CHUNK)
        w = jnp.exp2(mm(k[rows, :], q, NT) * SCALE2 + bias[rows, :] - lse)
        ds = (w * (mm(v[rows, :], u, NT) - delta)).astype(jnp.bfloat16)
        dv[rows, :] += mm(w.astype(jnp.bfloat16), u, NN)
        dk[rows, :] += mm(ds, q, NN)
        dq = dq + mm(kt[:, at : at + CHUNK], ds, NN)
    dq = (dq * FACTOR).T
    n = own_ref.shape[0]
    own_ref[...] = dq[:n]
    far_ref[...] = dq[n : 2 * n]
    core_ref[...] = dq[2 * n : 3 * n].astype(jnp.bfloat16)
    both_ref[...] = dq[3 * n :].astype(jnp.bfloat16)

    @pl.when(head == pl.num_programs(0) - 1)
    def _():
        terms_ref[:, :HEAD_DIM] = (dk[...] * FACTOR).astype(jnp.bfloat16)
        terms_ref[:, HEAD_DIM:] = dv[...].astype(jnp.bfloat16)


def split3(value):
    high = value.astype(jnp.bfloat16)
    rest = value - high.astype(jnp.float32)
    mid = rest.astype(jnp.bfloat16)
    low = (rest - mid.astype(jnp.float32)).astype(jnp.bfloat16)
    return high, mid, low


def upstream_kernel(order, *refs):
    parts, lse, w_hbm, out, w, sems = refs[:-5], *refs[-5:]
    width = parts[0].shape[1]
    copies = []
    for i in range(order.shape[0]):
        at = pl.multiple_of(order[i] * width, width)
        copies.append(pltpu.make_async_copy(w_hbm.at[:, pl.ds(at, width)], w.at[i], sems.at[i]))
        copies[-1].start()
    rows = out.shape[0] - EXTRA
    pieces = [piece for h in range(GROUPS) for piece in split3(lse[h])]
    pieces.append(jnp.zeros((EXTRA - len(pieces), out.shape[1]), jnp.bfloat16))
    out[rows:, :] = jnp.concatenate(pieces, axis=0)
    total, i = None, 0
    for part in parts:
        for at in range(0, part.shape[0], rows):
            copies[i].wait()
            term = mm(part[at : at + rows, :], w[i], NT)
            total = term if total is None else total + term
            i += 1
    out[:rows, :] = total.astype(out.dtype)


def whole(shape):
    return pl.BlockSpec(shape, lambda h: (0,) * len(shape))


def upstream_of(parts, order, lse, o_weight):
    width = parts[0].shape[1]
    cols = o_weight.shape[0]
    count = order.shape[0]
    rows = sum(p.shape[0] for p in parts) // count
    vmem = pl.BlockSpec(memory_space=pltpu.VMEM)
    return pl.pallas_call(
        upstream_kernel,
        out_shape=jax.ShapeDtypeStruct((rows + EXTRA, cols), jnp.bfloat16),
        in_specs=[pl.BlockSpec(memory_space=pltpu.SMEM)]
        + [vmem] * (len(parts) + 1)
        + [pl.BlockSpec(memory_space=pltpu.HBM)],
        out_specs=vmem,
        scratch_shapes=[
            pltpu.VMEM((count, cols, width), jnp.bfloat16),
            pltpu.SemaphoreType.DMA((count,)),
        ],
        compiler_params=pltpu.CompilerParams(vmem_limit_bytes=VMEM_LIMIT),
        name="upstream",
    )(order, *parts, lse, pltpu.with_memory_space_constraint(o_weight, pltpu.HBM))


def local(queries, key_states, value_states, out_grad, o_weight, span_order):
    rows = queries.shape[0]
    nz = lax.axis_size("z")
    nx = lax.axis_size("x")
    keys = nz * rows
    many = 4 * rows
    f32, bf16 = jnp.float32, jnp.bfloat16
    yh, z, c = lax.axis_index("yh"), lax.axis_index("z"), lax.axis_index("c")
    yl, x = lax.axis_index("yl"), lax.axis_index("x")

    both = jnp.concatenate((key_states, value_states), axis=1)
    kv = lax.all_to_all(
        jnp.broadcast_to(both[None], (nz, *both.shape)), "z", 0, 0, tiled=True
    ).reshape(keys, 2 * HEAD_DIM)

    pair = jnp.concatenate((out_grad, shift_by(out_grad, ("yl",), (1,))), axis=0)
    parts, sources = [], []
    for step in (0, 1, 3, 2):
        parts.append(shift_by(pair, ("x",), (step,)) if step else pair)
        near = (x - step) % nx
        sources += [yl * nx + near, (1 - yl) * nx + near]
    order = jnp.stack(sources).astype(jnp.int32)

    def shared(own):
        far = shift_by(own, ("yh",), (1,))
        return own, far, shift_by(own, ("c",), (1,)), shift_by(far, ("c",), (1,))

    def everyone(own):
        return (
            own,
            shift_by(own, ("yh",), (1,)),
            shift_by(own, ("c",), (1,)),
            shift_by(own, ("yh", "c"), (1, 1)),
        )

    spans = span_order.reshape(2, nz, 2, 2)
    offsets = jnp.arange(SPAN, dtype=jnp.int32)
    key_spans = lax.dynamic_slice(spans, (yh, 0, c, 0), (1, nz, 1, 2)).reshape(2 * nz, 1)
    kpos = (key_spans * SPAN + offsets[None, :]).reshape(keys, 1)
    groups = [(yh, c), (1 - yh, c), (yh, 1 - c), (1 - yh, 1 - c)]
    query_spans = jnp.concatenate(
        [lax.dynamic_slice(spans, (a, z, b, 0), (1, 1, 1, 2)).reshape(2, 1) for a, b in groups]
    )
    qpos = (query_spans * SPAN + offsets[None, :]).reshape(1, many)

    head_block = pl.BlockSpec((rows, HEAD_DIM), lambda h: (0, h))
    row_block = pl.BlockSpec((1, 1, many), lambda h: (h, 0, 0))
    row_shape = jax.ShapeDtypeStruct((GROUPS, 1, many), f32)
    places = [whole((keys, 1)), whole((1, many))]
    key_block = pl.BlockSpec((keys, HEAD_DIM), lambda h: (0, 0))
    value_block = pl.BlockSpec((keys, HEAD_DIM), lambda h: (0, 1))
    extra_block = pl.BlockSpec((EXTRA, many), lambda h: (rows // EXTRA, 0))
    term_sum = pltpu.VMEM((keys, HEAD_DIM), f32)
    bias = pltpu.VMEM((keys, many), f32)
    params = pltpu.CompilerParams(vmem_limit_bytes=VMEM_LIMIT)

    q = shared(queries)
    lse = pl.pallas_call(
        stats_kernel,
        grid=(GROUPS,),
        out_shape=row_shape,
        in_specs=places + [head_block] * 4 + [key_block],
        out_specs=row_block,
        scratch_shapes=[bias, bias],
        compiler_params=params,
        name="row_stats",
    )(kpos, qpos, *q, kv)

    upstream = upstream_of(parts, order, lse, o_weight)
    u = shared(upstream)
    lse_all, delta = pl.pallas_call(
        delta_kernel,
        grid=(GROUPS,),
        out_shape=(row_shape, row_shape),
        in_specs=places + [head_block] * 8 + [key_block, value_block] + [extra_block] * 4,
        out_specs=(row_block, row_block),
        scratch_shapes=[bias],
        compiler_params=params,
        name="row_delta",
    )(kpos, qpos, *q, *u, kv, kv, *u)
    delta_parts = everyone(delta)

    wide = (rows, GROUPS * HEAD_DIM)
    own, far, core, across, terms = pl.pallas_call(
        grad_kernel,
        grid=(GROUPS,),
        out_shape=(
            jax.ShapeDtypeStruct(wide, f32),
            jax.ShapeDtypeStruct(wide, f32),
            jax.ShapeDtypeStruct(wide, bf16),
            jax.ShapeDtypeStruct(wide, bf16),
            jax.ShapeDtypeStruct((keys, 2 * HEAD_DIM), bf16),
        ),
        in_specs=places
        + [head_block] * 8
        + [key_block, value_block]
        + [row_block] * 5,
        out_specs=(head_block,) * 4 + (whole((keys, 2 * HEAD_DIM)),),
        scratch_shapes=[bias, term_sum, term_sum, pltpu.VMEM((HEAD_DIM, keys), bf16)],
        compiler_params=params,
        name="gradients",
    )(kpos, qpos, *q, *u, kv, kv, lse_all, *delta_parts)

    summed = lax.all_to_all(terms.reshape(nz, rows, 2 * HEAD_DIM), "z", 0, 0, tiled=True)
    summed = jnp.sum(summed.astype(f32), axis=0)
    own = own + shift_by(core, ("c",), (1,)).astype(f32)
    far = far + shift_by(across, ("c",), (1,)).astype(f32)
    query_grad = own + shift_by(far.astype(bf16), ("yh",), (1,)).astype(f32)
    return query_grad, summed[:, :HEAD_DIM], summed[:, HEAD_DIM:]


def solution(mesh):
    finer = Mesh(mesh.devices.reshape(2, 8, 2, 2, 4), CP + VOCAB)
    return jax.shard_map(
        local,
        mesh=finer,
        in_specs=(P(CP, VOCAB), P(CP, VOCAB), P(CP, VOCAB), P(CP, VOCAB), P(VOCAB, None), P()),
        out_specs=(P(CP, VOCAB), P(CP, VOCAB), P(CP, VOCAB)),
        check_vma=False,
    )
```

```python
import math

import jax
import jax.numpy as jnp
from jax import lax
from jax.experimental import pallas as pl
from jax.experimental.pallas import tpu as pltpu
from jax.sharding import Mesh
from jax.sharding import PartitionSpec as P

HEADS = 32
KV_HEADS = 8
HEAD_DIM = 128
GROUPS = HEADS // KV_HEADS
SPAN = 64
CP = ("yh", "z", "c")
VOCAB = ("yl", "x")
FACTOR = HEAD_DIM**-0.5
SCALE2 = FACTOR * math.log2(math.e)
MASKED = -1e30
CHUNK = 256
VMEM_LIMIT = 32 * 1024 * 1024
NT = (((1,), (1,)), ((), ()))
NN = (((1,), (0,)), ((), ()))


def mm(a, b, dims):
    return lax.dot_general(a, b, dims, preferred_element_type=jnp.float32)


def shift_by(value, axes, steps):
    sizes = [lax.axis_size(a) for a in axes]
    total = math.prod(sizes)
    pairs = []
    for src in range(total):
        rest, at = src, []
        for n in reversed(sizes):
            at.insert(0, rest % n)
            rest //= n
        dst = 0
        for n, i, s in zip(sizes, at, steps):
            dst = dst * n + (i + s) % n
        pairs.append((src, dst))
    return lax.ppermute(value, axes, pairs)


def joined(refs):
    return jnp.concatenate([r[...] for r in refs], axis=0)


def fill_bias(kpos_ref, qpos_ref, bias_ref):
    @pl.when(pl.program_id(0) == 0)
    def _():
        for at in range(0, bias_ref.shape[0], CHUNK):
            rows = pl.ds(at, CHUNK)
            visible = kpos_ref[rows, :] <= qpos_ref[...]
            bias_ref[rows, :] = jnp.where(visible, 0.0, MASKED)


def stats_kernel(kpos, qpos, q0, q1, q2, q3, k, lse_ref, bias, s_scr):
    fill_bias(kpos, qpos, bias)
    q = joined((q0, q1, q2, q3))
    keys = k.shape[0]
    peak = jnp.full((1, q.shape[0]), MASKED, jnp.float32)
    for at in range(0, keys, CHUNK):
        rows = pl.ds(at, CHUNK)
        s = mm(k[rows, :], q, NT) * SCALE2 + bias[rows, :]
        s_scr[rows, :] = s
        peak = jnp.maximum(peak, jnp.max(s, axis=0, keepdims=True))
    total = jnp.zeros_like(peak)
    for at in range(0, keys, CHUNK):
        total = total + jnp.sum(jnp.exp2(s_scr[pl.ds(at, CHUNK), :] - peak), axis=0, keepdims=True)
    lse_ref[0] = peak + jnp.log2(total)


def aligned(own, far, core, both):
    n = own.shape[1] // 4

    def pick(a, order):
        return jnp.concatenate([a[:, g * n : (g + 1) * n] for g in order], axis=1)

    return own, pick(far, (1, 0, 3, 2)), pick(core, (2, 3, 0, 1)), pick(both, (3, 2, 1, 0))


def delta_kernel(
    kpos, qpos, q0, q1, q2, q3, u0, u1, u2, u3, k, v, lse_ref, stats_ref, bias
):
    fill_bias(kpos, qpos, bias)
    q, u = joined((q0, q1, q2, q3)), joined((u0, u1, u2, u3))
    lse = lse_ref[0]
    total = jnp.zeros_like(lse)
    for at in range(0, k.shape[0], CHUNK):
        rows = pl.ds(at, CHUNK)
        w = jnp.exp2(mm(k[rows, :], q, NT) * SCALE2 + bias[rows, :] - lse)
        total = total + jnp.sum(w * mm(v[rows, :], u, NT), axis=0, keepdims=True)
    stats_ref[0, 0:1, :] = lse
    stats_ref[0, 1:2, :] = total


def grad_kernel(
    kpos, qpos, q0, q1, q2, q3, u0, u1, u2, u3, k, v, s0, s1, s2, s3,
    own_ref, far_ref, core_ref, both_ref, terms_ref, bias, dk, dv, kt,
):
    fill_bias(kpos, qpos, bias)
    head = pl.program_id(0)
    q, u = joined((q0, q1, q2, q3)), joined((u0, u1, u2, u3))
    parts = aligned(s0[0], s1[0], s2[0], s3[0])
    peak = jnp.maximum(
        jnp.maximum(parts[0][:1], parts[1][:1]), jnp.maximum(parts[2][:1], parts[3][:1])
    )
    shares = [jnp.exp2(p[:1] - peak) for p in parts]
    whole_share = sum(shares)
    lse = peak + jnp.log2(whole_share)
    delta = sum(p[1:] * share for p, share in zip(parts, shares)) / whole_share

    @pl.when(head == 0)
    def _():
        dk[...] = jnp.zeros_like(dk)
        dv[...] = jnp.zeros_like(dv)
        kt[...] = k[...].T

    dq = jnp.zeros((HEAD_DIM, q.shape[0]), jnp.float32)
    for at in range(0, k.shape[0], CHUNK):
        rows = pl.ds(at, CHUNK)
        w = jnp.exp2(mm(k[rows, :], q, NT) * SCALE2 + bias[rows, :] - lse)
        ds = (w * (mm(v[rows, :], u, NT) - delta)).astype(jnp.bfloat16)
        dv[rows, :] += mm(w.astype(jnp.bfloat16), u, NN)
        dk[rows, :] += mm(ds, q, NN)
        dq = dq + mm(kt[:, at : at + CHUNK], ds, NN)
    dq = (dq * FACTOR).T
    n = own_ref.shape[0]
    own_ref[...] = dq[:n]
    far_ref[...] = dq[n : 2 * n]
    core_ref[...] = dq[2 * n : 3 * n].astype(jnp.bfloat16)
    both_ref[...] = dq[3 * n :].astype(jnp.bfloat16)

    @pl.when(head == pl.num_programs(0) - 1)
    def _():
        terms_ref[:, :HEAD_DIM] = (dk[...] * FACTOR).astype(jnp.bfloat16)
        terms_ref[:, HEAD_DIM:] = dv[...].astype(jnp.bfloat16)


def upstream_kernel(order, *refs):
    parts, w_hbm, out, w, sems = refs[:-4], *refs[-4:]
    rows, width = out.shape[0], parts[0].shape[1]
    copies = []
    for i in range(order.shape[0]):
        at = pl.multiple_of(order[i] * width, width)
        copies.append(pltpu.make_async_copy(w_hbm.at[:, pl.ds(at, width)], w.at[i], sems.at[i]))
        copies[-1].start()
    total, i = None, 0
    for part in parts:
        for at in range(0, part.shape[0], rows):
            copies[i].wait()
            term = mm(part[at : at + rows, :], w[i], NT)
            total = term if total is None else total + term
            i += 1
    out[...] = total.astype(out.dtype)


def upstream_of(parts, order, o_weight):
    width = parts[0].shape[1]
    cols = o_weight.shape[0]
    count = order.shape[0]
    rows = sum(p.shape[0] for p in parts) // count
    vmem = pl.BlockSpec(memory_space=pltpu.VMEM)
    return pl.pallas_call(
        upstream_kernel,
        out_shape=jax.ShapeDtypeStruct((rows, cols), jnp.bfloat16),
        in_specs=[pl.BlockSpec(memory_space=pltpu.SMEM)]
        + [vmem] * len(parts)
        + [pl.BlockSpec(memory_space=pltpu.HBM)],
        out_specs=vmem,
        scratch_shapes=[
            pltpu.VMEM((count, cols, width), jnp.bfloat16),
            pltpu.SemaphoreType.DMA((count,)),
        ],
        compiler_params=pltpu.CompilerParams(vmem_limit_bytes=VMEM_LIMIT),
        name="upstream",
    )(order, *parts, pltpu.with_memory_space_constraint(o_weight, pltpu.HBM))


def whole(shape):
    return pl.BlockSpec(shape, lambda h: (0,) * len(shape))


def local(queries, key_states, value_states, out_grad, o_weight, span_order):
    rows = queries.shape[0]
    nz = lax.axis_size("z")
    nx = lax.axis_size("x")
    keys = nz * rows
    many = 4 * rows
    f32, bf16 = jnp.float32, jnp.bfloat16
    yh, z, c = lax.axis_index("yh"), lax.axis_index("z"), lax.axis_index("c")
    yl, x = lax.axis_index("yl"), lax.axis_index("x")

    both = jnp.concatenate((key_states, value_states), axis=1)
    kv = lax.all_to_all(
        jnp.broadcast_to(both[None], (nz, *both.shape)), "z", 0, 0, tiled=True
    ).reshape(keys, 2 * HEAD_DIM)

    pair = jnp.concatenate((out_grad, shift_by(out_grad, ("yl",), (1,))), axis=0)
    parts, sources = [], []
    for step in (0, 1, 3, 2):
        parts.append(shift_by(pair, ("x",), (step,)) if step else pair)
        near = (x - step) % nx
        sources += [yl * nx + near, (1 - yl) * nx + near]
    order = jnp.stack(sources).astype(jnp.int32)

    def shared(own):
        far = shift_by(own, ("yh",), (1,))
        return own, far, shift_by(own, ("c",), (1,)), shift_by(far, ("c",), (1,))

    def everyone(own):
        return (
            own,
            shift_by(own, ("yh",), (1,)),
            shift_by(own, ("c",), (1,)),
            shift_by(own, ("yh", "c"), (1, 1)),
        )

    spans = span_order.reshape(2, nz, 2, 2)
    offsets = jnp.arange(SPAN, dtype=jnp.int32)
    key_spans = lax.dynamic_slice(spans, (yh, 0, c, 0), (1, nz, 1, 2)).reshape(2 * nz, 1)
    kpos = (key_spans * SPAN + offsets[None, :]).reshape(keys, 1)
    groups = [(yh, c), (1 - yh, c), (yh, 1 - c), (1 - yh, 1 - c)]
    query_spans = jnp.concatenate(
        [lax.dynamic_slice(spans, (a, z, b, 0), (1, 1, 1, 2)).reshape(2, 1) for a, b in groups]
    )
    qpos = (query_spans * SPAN + offsets[None, :]).reshape(1, many)

    head_block = pl.BlockSpec((rows, HEAD_DIM), lambda h: (0, h))
    row_block = pl.BlockSpec((1, 1, many), lambda h: (h, 0, 0))
    row_shape = jax.ShapeDtypeStruct((GROUPS, 1, many), f32)
    places = [whole((keys, 1)), whole((1, many))]
    key_block = pl.BlockSpec((keys, HEAD_DIM), lambda h: (0, 0))
    value_block = pl.BlockSpec((keys, HEAD_DIM), lambda h: (0, 1))
    stats_block = pl.BlockSpec((1, 2, many), lambda h: (h, 0, 0))
    term_sum = pltpu.VMEM((keys, HEAD_DIM), f32)
    bias = pltpu.VMEM((keys, many), f32)
    params = pltpu.CompilerParams(vmem_limit_bytes=VMEM_LIMIT)

    held, pair = lax.optimization_barrier((queries, pair))
    q = shared(held)
    lse = pl.pallas_call(
        stats_kernel,
        grid=(GROUPS,),
        out_shape=row_shape,
        in_specs=places + [head_block] * 4 + [key_block],
        out_specs=row_block,
        scratch_shapes=[bias, bias],
        compiler_params=params,
        name="row_stats",
    )(kpos, qpos, *q, kv)

    upstream = upstream_of(parts, order, o_weight)
    far = shift_by(upstream, ("yh",), (1,))
    far, lse = lax.optimization_barrier((far, lse))
    u = upstream, far, shift_by(upstream, ("c",), (1,)), shift_by(far, ("c",), (1,))
    stats = pl.pallas_call(
        delta_kernel,
        grid=(GROUPS,),
        out_shape=jax.ShapeDtypeStruct((GROUPS, 2, many), f32),
        in_specs=places + [head_block] * 8 + [key_block, value_block, row_block],
        out_specs=stats_block,
        scratch_shapes=[bias],
        compiler_params=params,
        name="row_delta",
    )(kpos, qpos, *q, *u, kv, kv, lse)
    stats_parts = everyone(stats)

    wide = (rows, GROUPS * HEAD_DIM)
    own, far, core, across, terms = pl.pallas_call(
        grad_kernel,
        grid=(GROUPS,),
        out_shape=(
            jax.ShapeDtypeStruct(wide, f32),
            jax.ShapeDtypeStruct(wide, f32),
            jax.ShapeDtypeStruct(wide, bf16),
            jax.ShapeDtypeStruct(wide, bf16),
            jax.ShapeDtypeStruct((keys, 2 * HEAD_DIM), bf16),
        ),
        in_specs=places
        + [head_block] * 8
        + [key_block, value_block]
        + [stats_block] * 4,
        out_specs=(head_block,) * 4 + (whole((keys, 2 * HEAD_DIM)),),
        scratch_shapes=[bias, term_sum, term_sum, pltpu.VMEM((HEAD_DIM, keys), bf16)],
        compiler_params=params,
        name="gradients",
    )(kpos, qpos, *q, *u, kv, kv, *stats_parts)

    summed = lax.all_to_all(terms.reshape(nz, rows, 2 * HEAD_DIM), "z", 0, 0, tiled=True)
    summed = jnp.sum(summed.astype(f32), axis=0)
    own = own + shift_by(core, ("c",), (1,)).astype(f32)
    far = far + shift_by(across, ("c",), (1,)).astype(f32)
    query_grad = own + shift_by(far.astype(bf16), ("yh",), (1,)).astype(f32)
    return query_grad, summed[:, :HEAD_DIM], summed[:, HEAD_DIM:]


def solution(mesh):
    finer = Mesh(mesh.devices.reshape(2, 8, 2, 2, 4), CP + VOCAB)
    return jax.shard_map(
        local,
        mesh=finer,
        in_specs=(P(CP, VOCAB), P(CP, VOCAB), P(CP, VOCAB), P(CP, VOCAB), P(VOCAB, None), P()),
        out_specs=(P(CP, VOCAB), P(CP, VOCAB), P(CP, VOCAB)),
        check_vma=False,
    )
```

```python
import math

import jax
import jax.numpy as jnp
from jax import lax
from jax.experimental import pallas as pl
from jax.experimental.pallas import tpu as pltpu
from jax.sharding import Mesh
from jax.sharding import PartitionSpec as P

HEADS = 32
KV_HEADS = 8
HEAD_DIM = 128
GROUPS = HEADS // KV_HEADS
SPAN = 64
CP = ("yh", "z", "c")
VOCAB = ("yl", "x")
FACTOR = HEAD_DIM**-0.5
SCALE2 = FACTOR * math.log2(math.e)
MASKED = -1e30
CHUNK = 512
VMEM_LIMIT = 32 * 1024 * 1024
NT = (((1,), (1,)), ((), ()))
NN = (((1,), (0,)), ((), ()))


def mm(a, b, dims):
    return lax.dot_general(a, b, dims, preferred_element_type=jnp.float32)


def shift_by(value, axes, steps):
    sizes = [lax.axis_size(a) for a in axes]
    total = math.prod(sizes)
    pairs = []
    for src in range(total):
        rest, at = src, []
        for n in reversed(sizes):
            at.insert(0, rest % n)
            rest //= n
        dst = 0
        for n, i, s in zip(sizes, at, steps):
            dst = dst * n + (i + s) % n
        pairs.append((src, dst))
    return lax.ppermute(value, axes, pairs)


def by_heads(refs):
    return jnp.concatenate(
        [r[:, h * HEAD_DIM : (h + 1) * HEAD_DIM] for h in range(GROUPS) for r in refs], axis=0
    )


def chunk_scores(k, kpos, qpos, q, at):
    rows = pl.ds(at, CHUNK)
    bias = jnp.where(kpos[rows, :] <= qpos[...], 0.0, MASKED)
    bias = jnp.concatenate([bias] * GROUPS, axis=1)
    return mm(k[rows, :HEAD_DIM], q, NT) * SCALE2 + bias


def stats_kernel(kpos, qpos, q0, q1, q2, q3, kv, lse_ref, q_scr, s_scr):
    q_scr[...] = by_heads((q0, q1, q2, q3))
    keys = kv.shape[0]
    peak = jnp.full((1, q_scr.shape[0]), MASKED, jnp.float32)
    for at in range(0, keys, CHUNK):
        s = chunk_scores(kv, kpos, qpos, q_scr[...], at)
        s_scr[pl.ds(at, CHUNK), :] = s
        peak = jnp.maximum(peak, jnp.max(s, axis=0, keepdims=True))
    total = jnp.zeros_like(peak)
    for at in range(0, keys, CHUNK):
        total = total + jnp.sum(jnp.exp2(s_scr[pl.ds(at, CHUNK), :] - peak), axis=0, keepdims=True)
    lse_ref[...] = peak + jnp.log2(total)


def aligned(own, far, core, both):
    n = own.shape[1] // (4 * GROUPS)

    def pick(a, order):
        return jnp.concatenate(
            [a[:, (4 * h + g) * n : (4 * h + g + 1) * n] for h in range(GROUPS) for g in order],
            axis=1,
        )

    return own, pick(far, (1, 0, 3, 2)), pick(core, (2, 3, 0, 1)), pick(both, (3, 2, 1, 0))


def delta_kernel(
    kpos, qpos, q0, q1, q2, q3, u0, u1, u2, u3, kv, lse_ref, stats_ref, q_scr, u_scr
):
    q_scr[...] = by_heads((q0, q1, q2, q3))
    u_scr[...] = by_heads((u0, u1, u2, u3))
    lse = lse_ref[...]
    total = jnp.zeros_like(lse)
    for at in range(0, kv.shape[0], CHUNK):
        w = jnp.exp2(chunk_scores(kv, kpos, qpos, q_scr[...], at) - lse)
        dp = mm(kv[pl.ds(at, CHUNK), HEAD_DIM:], u_scr[...], NT)
        total = total + jnp.sum(w * dp, axis=0, keepdims=True)
    stats_ref[0:1, :] = lse
    stats_ref[1:2, :] = total


def grad_kernel(
    kpos, qpos, q0, q1, q2, q3, u0, u1, u2, u3, kv, s0, s1, s2, s3,
    own_ref, far_ref, core_ref, both_ref, terms_ref, q_scr, u_scr, dq_scr,
):
    q_scr[...] = by_heads((q0, q1, q2, q3))
    u_scr[...] = by_heads((u0, u1, u2, u3))
    parts = aligned(s0[...], s1[...], s2[...], s3[...])
    peak = jnp.maximum(
        jnp.maximum(parts[0][:1], parts[1][:1]), jnp.maximum(parts[2][:1], parts[3][:1])
    )
    shares = [jnp.exp2(p[:1] - peak) for p in parts]
    whole_share = sum(shares)
    lse = peak + jnp.log2(whole_share)
    delta = sum(p[1:] * share for p, share in zip(parts, shares)) / whole_share

    for at in range(0, kv.shape[0], CHUNK):
        rows = pl.ds(at, CHUNK)
        w = jnp.exp2(chunk_scores(kv, kpos, qpos, q_scr[...], at) - lse)
        dp = mm(kv[rows, HEAD_DIM:], u_scr[...], NT)
        ds = (w * (dp - delta)).astype(jnp.bfloat16)
        terms_ref[rows, HEAD_DIM:] = mm(w.astype(jnp.bfloat16), u_scr[...], NN).astype(jnp.bfloat16)
        terms_ref[rows, :HEAD_DIM] = (mm(ds, q_scr[...], NN) * FACTOR).astype(jnp.bfloat16)
        dq = mm(kv[rows, :HEAD_DIM].T, ds, NN)
        dq_scr[...] = dq if at == 0 else dq_scr[...] + dq
    n = own_ref.shape[0]
    for h in range(GROUPS):
        for g, ref in enumerate((own_ref, far_ref, core_ref, both_ref)):
            at = (4 * h + g) * n
            part = (dq_scr[:, at : at + n] * FACTOR).T
            ref[:, h * HEAD_DIM : (h + 1) * HEAD_DIM] = part.astype(ref.dtype)


def upstream_kernel(order, *refs):
    parts, w_hbm, out, w, sems = refs[:-4], *refs[-4:]
    rows, width = out.shape[0], parts[0].shape[1]
    copies = []
    for i in range(order.shape[0]):
        at = pl.multiple_of(order[i] * width, width)
        copies.append(pltpu.make_async_copy(w_hbm.at[:, pl.ds(at, width)], w.at[i], sems.at[i]))
        copies[-1].start()
    total, i = None, 0
    for part in parts:
        for at in range(0, part.shape[0], rows):
            copies[i].wait()
            term = mm(part[at : at + rows, :], w[i], NT)
            total = term if total is None else total + term
            i += 1
    out[...] = total.astype(out.dtype)


def upstream_of(parts, order, o_weight):
    width = parts[0].shape[1]
    cols = o_weight.shape[0]
    count = order.shape[0]
    rows = sum(p.shape[0] for p in parts) // count
    vmem = pl.BlockSpec(memory_space=pltpu.VMEM)
    return pl.pallas_call(
        upstream_kernel,
        out_shape=jax.ShapeDtypeStruct((rows, cols), jnp.bfloat16),
        in_specs=[pl.BlockSpec(memory_space=pltpu.SMEM)]
        + [vmem] * len(parts)
        + [pl.BlockSpec(memory_space=pltpu.HBM)],
        out_specs=vmem,
        scratch_shapes=[
            pltpu.VMEM((count, cols, width), jnp.bfloat16),
            pltpu.SemaphoreType.DMA((count,)),
        ],
        compiler_params=pltpu.CompilerParams(vmem_limit_bytes=VMEM_LIMIT),
        name="upstream",
    )(order, *parts, pltpu.with_memory_space_constraint(o_weight, pltpu.HBM))


def local(queries, key_states, value_states, out_grad, o_weight, span_order):
    rows = queries.shape[0]
    nz = lax.axis_size("z")
    nx = lax.axis_size("x")
    keys = nz * rows
    many = 4 * rows
    f32, bf16 = jnp.float32, jnp.bfloat16
    yh, z, c = lax.axis_index("yh"), lax.axis_index("z"), lax.axis_index("c")
    yl, x = lax.axis_index("yl"), lax.axis_index("x")

    both = jnp.concatenate((key_states, value_states), axis=1)
    kv = lax.all_to_all(
        jnp.broadcast_to(both[None], (nz, *both.shape)), "z", 0, 0, tiled=True
    ).reshape(keys, 2 * HEAD_DIM)

    pair = jnp.concatenate((out_grad, shift_by(out_grad, ("yl",), (1,))), axis=0)
    parts, sources = [], []
    for step in (0, 1, 3, 2):
        parts.append(shift_by(pair, ("x",), (step,)) if step else pair)
        near = (x - step) % nx
        sources += [yl * nx + near, (1 - yl) * nx + near]
    order = jnp.stack(sources).astype(jnp.int32)

    def shared(own):
        far = shift_by(own, ("yh",), (1,))
        return own, far, shift_by(own, ("c",), (1,)), shift_by(far, ("c",), (1,))

    def everyone(own):
        return (
            own,
            shift_by(own, ("yh",), (1,)),
            shift_by(own, ("c",), (1,)),
            shift_by(own, ("yh", "c"), (1, 1)),
        )

    spans = span_order.reshape(2, nz, 2, 2)
    offsets = jnp.arange(SPAN, dtype=jnp.int32)
    key_spans = lax.dynamic_slice(spans, (yh, 0, c, 0), (1, nz, 1, 2)).reshape(2 * nz, 1)
    kpos = (key_spans * SPAN + offsets[None, :]).reshape(keys, 1)
    groups = [(yh, c), (1 - yh, c), (yh, 1 - c), (1 - yh, 1 - c)]
    query_spans = jnp.concatenate(
        [lax.dynamic_slice(spans, (a, z, b, 0), (1, 1, 1, 2)).reshape(2, 1) for a, b in groups]
    )
    qpos = (query_spans * SPAN + offsets[None, :]).reshape(1, many)

    vmem = pl.BlockSpec(memory_space=pltpu.VMEM)
    wide = pltpu.VMEM((GROUPS * many, HEAD_DIM), bf16)
    params = pltpu.CompilerParams(vmem_limit_bytes=VMEM_LIMIT)

    held, pair = lax.optimization_barrier((queries, pair))
    q = shared(held)
    lse = pl.pallas_call(
        stats_kernel,
        out_shape=jax.ShapeDtypeStruct((1, GROUPS * many), f32),
        in_specs=[vmem] * 7,
        out_specs=vmem,
        scratch_shapes=[wide, pltpu.VMEM((keys, GROUPS * many), f32)],
        compiler_params=params,
        name="row_stats",
    )(kpos, qpos, *q, kv)

    upstream = upstream_of(parts, order, o_weight)
    far = shift_by(upstream, ("yh",), (1,))
    far, lse = lax.optimization_barrier((far, lse))
    u = upstream, far, shift_by(upstream, ("c",), (1,)), shift_by(far, ("c",), (1,))
    stats = pl.pallas_call(
        delta_kernel,
        out_shape=jax.ShapeDtypeStruct((2, GROUPS * many), f32),
        in_specs=[vmem] * 12,
        out_specs=vmem,
        scratch_shapes=[wide, wide],
        compiler_params=params,
        name="row_delta",
    )(kpos, qpos, *q, *u, kv, lse)
    stats_parts = everyone(stats)

    shape = (rows, GROUPS * HEAD_DIM)
    own, far, core, across, terms = pl.pallas_call(
        grad_kernel,
        out_shape=(
            jax.ShapeDtypeStruct(shape, f32),
            jax.ShapeDtypeStruct(shape, f32),
            jax.ShapeDtypeStruct(shape, bf16),
            jax.ShapeDtypeStruct(shape, bf16),
            jax.ShapeDtypeStruct((keys, 2 * HEAD_DIM), bf16),
        ),
        in_specs=[vmem] * 15,
        out_specs=(vmem,) * 5,
        scratch_shapes=[wide, wide, pltpu.VMEM((HEAD_DIM, GROUPS * many), f32)],
        compiler_params=params,
        name="gradients",
    )(kpos, qpos, *q, *u, kv, *stats_parts)

    summed = lax.all_to_all(terms.reshape(nz, rows, 2 * HEAD_DIM), "z", 0, 0, tiled=True)
    summed = jnp.sum(summed.astype(f32), axis=0)
    own = own + shift_by(core, ("c",), (1,)).astype(f32)
    far = far + shift_by(across, ("c",), (1,)).astype(f32)
    query_grad = own + shift_by(far.astype(bf16), ("yh",), (1,)).astype(f32)
    return query_grad, summed[:, :HEAD_DIM], summed[:, HEAD_DIM:]


def solution(mesh):
    finer = Mesh(mesh.devices.reshape(2, 8, 2, 2, 4), CP + VOCAB)
    return jax.shard_map(
        local,
        mesh=finer,
        in_specs=(P(CP, VOCAB), P(CP, VOCAB), P(CP, VOCAB), P(CP, VOCAB), P(VOCAB, None), P()),
        out_specs=(P(CP, VOCAB), P(CP, VOCAB), P(CP, VOCAB)),
        check_vma=False,
    )
```

```python
import math

import jax
import jax.numpy as jnp
from jax import lax
from jax.experimental import pallas as pl
from jax.experimental.pallas import tpu as pltpu
from jax.sharding import Mesh
from jax.sharding import PartitionSpec as P

HEADS = 32
KV_HEADS = 8
HEAD_DIM = 128
GROUPS = HEADS // KV_HEADS
SPAN = 64
CP = ("yh", "z", "c")
VOCAB = ("yl", "x")
FACTOR = HEAD_DIM**-0.5
SCALE2 = FACTOR * math.log2(math.e)
MASKED = -1e30
CHUNK = 512
VMEM_LIMIT = 32 * 1024 * 1024
NT = (((1,), (1,)), ((), ()))
NN = (((1,), (0,)), ((), ()))


def mm(a, b, dims):
    return lax.dot_general(a, b, dims, preferred_element_type=jnp.float32)


def shift_by(value, axes, steps):
    sizes = [lax.axis_size(a) for a in axes]
    total = math.prod(sizes)
    pairs = []
    for src in range(total):
        rest, at = src, []
        for n in reversed(sizes):
            at.insert(0, rest % n)
            rest //= n
        dst = 0
        for n, i, s in zip(sizes, at, steps):
            dst = dst * n + (i + s) % n
        pairs.append((src, dst))
    return lax.ppermute(value, axes, pairs)


def by_heads(refs):
    return jnp.concatenate(
        [r[:, h * HEAD_DIM : (h + 1) * HEAD_DIM] for h in range(GROUPS) for r in refs], axis=0
    )


def chunk_scores(k, kpos, qpos, q, at):
    rows = pl.ds(at, CHUNK)
    bias = jnp.where(kpos[rows, :] <= qpos[...], 0.0, MASKED)
    bias = jnp.concatenate([bias] * GROUPS, axis=1)
    return mm(k[rows, :HEAD_DIM], q, NT) * SCALE2 + bias


def stats_kernel(kpos, qpos, q0, q1, q2, q3, kv, lse_ref, q_scr, s_scr):
    q_scr[...] = by_heads((q0, q1, q2, q3))
    keys = kv.shape[0]
    peak = jnp.full((1, q_scr.shape[0]), MASKED, jnp.float32)
    for at in range(0, keys, CHUNK):
        s = chunk_scores(kv, kpos, qpos, q_scr[...], at)
        s_scr[pl.ds(at, CHUNK), :] = s
        peak = jnp.maximum(peak, jnp.max(s, axis=0, keepdims=True))
    total = jnp.zeros_like(peak)
    for at in range(0, keys, CHUNK):
        total = total + jnp.sum(jnp.exp2(s_scr[pl.ds(at, CHUNK), :] - peak), axis=0, keepdims=True)
    lse_ref[...] = peak + jnp.log2(total)


def aligned(own, far, core, both):
    n = own.shape[1] // (4 * GROUPS)

    def pick(a, order):
        return jnp.concatenate(
            [a[:, (4 * h + g) * n : (4 * h + g + 1) * n] for h in range(GROUPS) for g in order],
            axis=1,
        )

    return own, pick(far, (1, 0, 3, 2)), pick(core, (2, 3, 0, 1)), pick(both, (3, 2, 1, 0))


def delta_kernel(
    kpos, qpos, q0, q1, q2, q3, u0, u1, u2, u3, kv, lse_ref, stats_ref, q_scr, u_scr
):
    q_scr[...] = by_heads((q0, q1, q2, q3))
    u_scr[...] = by_heads((u0, u1, u2, u3))
    lse = lse_ref[...]
    total = jnp.zeros_like(lse)
    for at in range(0, kv.shape[0], CHUNK):
        w = jnp.exp2(chunk_scores(kv, kpos, qpos, q_scr[...], at) - lse)
        dp = mm(kv[pl.ds(at, CHUNK), HEAD_DIM:], u_scr[...], NT)
        total = total + jnp.sum(w * dp, axis=0, keepdims=True)
    stats_ref[0:1, :] = lse
    stats_ref[1:2, :] = total


def grad_kernel(
    kpos, qpos, q0, q1, q2, q3, u0, u1, u2, u3, kv, s0, s1, s2, s3,
    own_ref, far_ref, core_ref, both_ref, terms_ref, q_scr, u_scr, dq_scr,
):
    q_scr[...] = by_heads((q0, q1, q2, q3))
    u_scr[...] = by_heads((u0, u1, u2, u3))
    parts = aligned(s0[...], s1[...], s2[...], s3[...])
    peak = jnp.maximum(
        jnp.maximum(parts[0][:1], parts[1][:1]), jnp.maximum(parts[2][:1], parts[3][:1])
    )
    shares = [jnp.exp2(p[:1] - peak) for p in parts]
    whole_share = sum(shares)
    lse = peak + jnp.log2(whole_share)
    delta = sum(p[1:] * share for p, share in zip(parts, shares)) / whole_share

    for at in range(0, kv.shape[0], CHUNK):
        rows = pl.ds(at, CHUNK)
        w = jnp.exp2(chunk_scores(kv, kpos, qpos, q_scr[...], at) - lse)
        dp = mm(kv[rows, HEAD_DIM:], u_scr[...], NT)
        ds = (w * (dp - delta)).astype(jnp.bfloat16)
        terms_ref[rows, HEAD_DIM:] = mm(w.astype(jnp.bfloat16), u_scr[...], NN).astype(jnp.bfloat16)
        terms_ref[rows, :HEAD_DIM] = (mm(ds, q_scr[...], NN) * FACTOR).astype(jnp.bfloat16)
        dq = mm(kv[rows, :HEAD_DIM].T, ds, NN)
        dq_scr[...] = dq if at == 0 else dq_scr[...] + dq
    n = own_ref.shape[0]
    for h in range(GROUPS):
        for g, ref in enumerate((own_ref, far_ref, core_ref, both_ref)):
            at = (4 * h + g) * n
            part = (dq_scr[:, at : at + n] * FACTOR).T
            ref[:, h * HEAD_DIM : (h + 1) * HEAD_DIM] = part.astype(ref.dtype)


def upstream_kernel(order, *refs):
    parts, w_hbm, out, w, sems = refs[:-4], *refs[-4:]
    rows, width = out.shape[0], parts[0].shape[1]
    copies = []
    for i in range(order.shape[0]):
        at = pl.multiple_of(order[i] * width, width)
        copies.append(pltpu.make_async_copy(w_hbm.at[:, pl.ds(at, width)], w.at[i], sems.at[i]))
        copies[-1].start()
    total, i = None, 0
    for part in parts:
        for at in range(0, part.shape[0], rows):
            copies[i].wait()
            term = mm(part[at : at + rows, :], w[i], NT)
            total = term if total is None else total + term
            i += 1
    out[...] = total.astype(out.dtype)


def upstream_of(parts, order, o_weight):
    width = parts[0].shape[1]
    cols = o_weight.shape[0]
    count = order.shape[0]
    rows = sum(p.shape[0] for p in parts) // count
    vmem = pl.BlockSpec(memory_space=pltpu.VMEM)
    return pl.pallas_call(
        upstream_kernel,
        out_shape=jax.ShapeDtypeStruct((rows, cols), jnp.bfloat16),
        in_specs=[pl.BlockSpec(memory_space=pltpu.SMEM)]
        + [vmem] * len(parts)
        + [pl.BlockSpec(memory_space=pltpu.HBM)],
        out_specs=vmem,
        scratch_shapes=[
            pltpu.VMEM((count, cols, width), jnp.bfloat16),
            pltpu.SemaphoreType.DMA((count,)),
        ],
        compiler_params=pltpu.CompilerParams(vmem_limit_bytes=VMEM_LIMIT),
        name="upstream",
    )(order, *parts, pltpu.with_memory_space_constraint(o_weight, pltpu.HBM))


def pack_kernel(k, v, out):
    rows = k.shape[0]
    for at in range(0, out.shape[0], rows):
        out[at : at + rows, :HEAD_DIM] = k[...]
        out[at : at + rows, HEAD_DIM:] = v[...]


def packed(key_states, value_states, copies):
    rows, width = key_states.shape
    vmem = pl.BlockSpec(memory_space=pltpu.VMEM)
    return pl.pallas_call(
        pack_kernel,
        out_shape=jax.ShapeDtypeStruct((copies * rows, 2 * width), key_states.dtype),
        in_specs=[vmem, vmem],
        out_specs=vmem,
        cost_estimate=pl.CostEstimate(flops=0, transcendentals=0, bytes_accessed=12 * key_states.size),
        name="pack",
    )(key_states, value_states)


def local(queries, key_states, value_states, out_grad, o_weight, span_order):
    rows = queries.shape[0]
    nz = lax.axis_size("z")
    nx = lax.axis_size("x")
    keys = nz * rows
    many = 4 * rows
    f32, bf16 = jnp.float32, jnp.bfloat16
    yh, z, c = lax.axis_index("yh"), lax.axis_index("z"), lax.axis_index("c")
    yl, x = lax.axis_index("yl"), lax.axis_index("x")

    both = packed(key_states, value_states, nz).reshape(nz, rows, 2 * HEAD_DIM)
    kv = lax.all_to_all(both, "z", 0, 0, tiled=True).reshape(keys, 2 * HEAD_DIM)

    pair = jnp.concatenate((out_grad, shift_by(out_grad, ("yl",), (1,))), axis=0)
    parts, sources = [], []
    for step in (0, 1, 3, 2):
        parts.append(shift_by(pair, ("x",), (step,)) if step else pair)
        near = (x - step) % nx
        sources += [yl * nx + near, (1 - yl) * nx + near]
    order = jnp.stack(sources).astype(jnp.int32)

    def shared(own):
        far = shift_by(own, ("yh",), (1,))
        return own, far, shift_by(own, ("c",), (1,)), shift_by(far, ("c",), (1,))

    def everyone(own):
        return (
            own,
            shift_by(own, ("yh",), (1,)),
            shift_by(own, ("c",), (1,)),
            shift_by(own, ("yh", "c"), (1, 1)),
        )

    spans = span_order.reshape(2, nz, 2, 2)
    offsets = jnp.arange(SPAN, dtype=jnp.int32)
    key_spans = lax.dynamic_slice(spans, (yh, 0, c, 0), (1, nz, 1, 2)).reshape(2 * nz, 1)
    kpos = (key_spans * SPAN + offsets[None, :]).reshape(keys, 1)
    groups = [(yh, c), (1 - yh, c), (yh, 1 - c), (1 - yh, 1 - c)]
    query_spans = jnp.concatenate(
        [lax.dynamic_slice(spans, (a, z, b, 0), (1, 1, 1, 2)).reshape(2, 1) for a, b in groups]
    )
    qpos = (query_spans * SPAN + offsets[None, :]).reshape(1, many)

    vmem = pl.BlockSpec(memory_space=pltpu.VMEM)
    wide = pltpu.VMEM((GROUPS * many, HEAD_DIM), bf16)
    params = pltpu.CompilerParams(vmem_limit_bytes=VMEM_LIMIT)

    held, pair, kpos, qpos = lax.optimization_barrier((queries, pair, kpos, qpos))
    q = shared(held)
    lse = pl.pallas_call(
        stats_kernel,
        out_shape=jax.ShapeDtypeStruct((1, GROUPS * many), f32),
        in_specs=[vmem] * 7,
        out_specs=vmem,
        scratch_shapes=[wide, pltpu.VMEM((keys, GROUPS * many), f32)],
        compiler_params=params,
        name="row_stats",
    )(kpos, qpos, *q, kv)

    upstream = upstream_of(parts, order, o_weight)
    far = shift_by(upstream, ("yh",), (1,))
    far, lse = lax.optimization_barrier((far, lse))
    u = upstream, far, shift_by(upstream, ("c",), (1,)), shift_by(far, ("c",), (1,))
    stats = pl.pallas_call(
        delta_kernel,
        out_shape=jax.ShapeDtypeStruct((2, GROUPS * many), f32),
        in_specs=[vmem] * 12,
        out_specs=vmem,
        scratch_shapes=[wide, wide],
        compiler_params=params,
        name="row_delta",
    )(kpos, qpos, *q, *u, kv, lse)
    stats_parts = everyone(stats)

    shape = (rows, GROUPS * HEAD_DIM)
    own, far, core, across, terms = pl.pallas_call(
        grad_kernel,
        out_shape=(
            jax.ShapeDtypeStruct(shape, f32),
            jax.ShapeDtypeStruct(shape, f32),
            jax.ShapeDtypeStruct(shape, bf16),
            jax.ShapeDtypeStruct(shape, bf16),
            jax.ShapeDtypeStruct((keys, 2 * HEAD_DIM), bf16),
        ),
        in_specs=[vmem] * 15,
        out_specs=(vmem,) * 5,
        scratch_shapes=[wide, wide, pltpu.VMEM((HEAD_DIM, GROUPS * many), f32)],
        compiler_params=params,
        name="gradients",
    )(kpos, qpos, *q, *u, kv, *stats_parts)

    summed = lax.all_to_all(terms.reshape(nz, rows, 2 * HEAD_DIM), "z", 0, 0, tiled=True)
    summed = jnp.sum(summed.astype(f32), axis=0)
    own = own + shift_by(core, ("c",), (1,)).astype(f32)
    far = far + shift_by(across, ("c",), (1,)).astype(f32)
    query_grad = own + shift_by(far.astype(bf16), ("yh",), (1,)).astype(f32)
    return query_grad, summed[:, :HEAD_DIM], summed[:, HEAD_DIM:]


def solution(mesh):
    finer = Mesh(mesh.devices.reshape(2, 8, 2, 2, 4), CP + VOCAB)
    return jax.shard_map(
        local,
        mesh=finer,
        in_specs=(P(CP, VOCAB), P(CP, VOCAB), P(CP, VOCAB), P(CP, VOCAB), P(VOCAB, None), P()),
        out_specs=(P(CP, VOCAB), P(CP, VOCAB), P(CP, VOCAB)),
        check_vma=False,
    )
```

```python
import math

import jax
import jax.numpy as jnp
from jax import lax
from jax.experimental import pallas as pl
from jax.experimental.pallas import tpu as pltpu
from jax.sharding import Mesh
from jax.sharding import PartitionSpec as P

HEADS = 32
KV_HEADS = 8
HEAD_DIM = 128
GROUPS = HEADS // KV_HEADS
SPAN = 64
CP = ("yh", "z", "c")
VOCAB = ("yl", "x")
FACTOR = HEAD_DIM**-0.5
SCALE2 = FACTOR * math.log2(math.e)
MASKED = -1e30
CHUNK = 512
VMEM_LIMIT = 32 * 1024 * 1024
NT = (((1,), (1,)), ((), ()))
NN = (((1,), (0,)), ((), ()))


def mm(a, b, dims):
    return lax.dot_general(a, b, dims, preferred_element_type=jnp.float32)


def shift_by(value, axes, steps):
    sizes = [lax.axis_size(a) for a in axes]
    total = math.prod(sizes)
    pairs = []
    for src in range(total):
        rest, at = src, []
        for n in reversed(sizes):
            at.insert(0, rest % n)
            rest //= n
        dst = 0
        for n, i, s in zip(sizes, at, steps):
            dst = dst * n + (i + s) % n
        pairs.append((src, dst))
    return lax.ppermute(value, axes, pairs)


def by_heads(refs):
    return jnp.concatenate(
        [r[:, h * HEAD_DIM : (h + 1) * HEAD_DIM] for h in range(GROUPS) for r in refs], axis=0
    )


def chunk_scores(k, kpos, qpos, q, at):
    rows = pl.ds(at, CHUNK)
    bias = jnp.where(kpos[rows, :] <= qpos[...], 0.0, MASKED)
    bias = jnp.concatenate([bias] * GROUPS, axis=1)
    return mm(k[rows, :HEAD_DIM], q, NT) * SCALE2 + bias


def stats_kernel(kpos, qpos, q0, q1, q2, q3, kv, lse_ref, q_scr, s_scr):
    q_scr[...] = by_heads((q0, q1, q2, q3))
    keys = kv.shape[0]
    peak = jnp.full((1, q_scr.shape[0]), MASKED, jnp.float32)
    for at in range(0, keys, CHUNK):
        s = chunk_scores(kv, kpos, qpos, q_scr[...], at)
        s_scr[pl.ds(at, CHUNK), :] = s
        peak = jnp.maximum(peak, jnp.max(s, axis=0, keepdims=True))
    total = jnp.zeros_like(peak)
    for at in range(0, keys, CHUNK):
        total = total + jnp.sum(jnp.exp2(s_scr[pl.ds(at, CHUNK), :] - peak), axis=0, keepdims=True)
    lse_ref[...] = peak + jnp.log2(total)


def aligned(own, far, core, both):
    n = own.shape[1] // (4 * GROUPS)

    def pick(a, order):
        return jnp.concatenate(
            [a[:, (4 * h + g) * n : (4 * h + g + 1) * n] for h in range(GROUPS) for g in order],
            axis=1,
        )

    return own, pick(far, (1, 0, 3, 2)), pick(core, (2, 3, 0, 1)), pick(both, (3, 2, 1, 0))


def half_delta(kpos, qpos, q_refs, u_refs, kv, lse, q_scr, u_scr, groups):
    n = qpos.shape[1] // 4
    q_scr[...] = by_heads(q_refs)
    u_scr[...] = by_heads(u_refs)
    places = jnp.concatenate([qpos[:, g * n : (g + 1) * n] for g in groups], axis=1)
    lse = jnp.concatenate(
        [lse[:, (4 * h + g) * n : (4 * h + g + 1) * n] for h in range(GROUPS) for g in groups],
        axis=1,
    )
    total = jnp.zeros_like(lse)
    for at in range(0, kv.shape[0], CHUNK):
        w = jnp.exp2(chunk_scores(kv, kpos, places, q_scr[...], at) - lse)
        dp = mm(kv[pl.ds(at, CHUNK), HEAD_DIM:], u_scr[...], NT)
        total = total + jnp.sum(w * dp, axis=0, keepdims=True)
    return total


def near_delta_kernel(kpos, qpos, q0, q2, u0, u2, kv, lse, out, q_scr, u_scr):
    out[...] = half_delta(kpos, qpos, (q0, q2), (u0, u2), kv, lse, q_scr, u_scr, (0, 2))


def far_delta_kernel(kpos, qpos, q1, q3, u1, u3, kv, lse, near, stats_ref, q_scr, u_scr):
    far = half_delta(kpos, qpos, (q1, q3), (u1, u3), kv, lse, q_scr, u_scr, (1, 3))
    n = qpos.shape[1] // 4
    stats_ref[0:1, :] = lse[...]
    for h in range(GROUPS):
        for g in range(4):
            half = far[:, :] if g % 2 else near[...]
            at = 2 * h + g // 2
            stats_ref[1:2, (4 * h + g) * n : (4 * h + g + 1) * n] = half[:, at * n : (at + 1) * n]


def grad_kernel(
    kpos, qpos, q0, q1, q2, q3, u0, u1, u2, u3, kv, s0, s1, s2, s3,
    own_ref, far_ref, core_ref, both_ref, terms_ref, q_scr, u_scr, dq_scr,
):
    q_scr[...] = by_heads((q0, q1, q2, q3))
    u_scr[...] = by_heads((u0, u1, u2, u3))
    parts = aligned(s0[...], s1[...], s2[...], s3[...])
    peak = jnp.maximum(
        jnp.maximum(parts[0][:1], parts[1][:1]), jnp.maximum(parts[2][:1], parts[3][:1])
    )
    shares = [jnp.exp2(p[:1] - peak) for p in parts]
    whole_share = sum(shares)
    lse = peak + jnp.log2(whole_share)
    delta = sum(p[1:] * share for p, share in zip(parts, shares)) / whole_share

    for at in range(0, kv.shape[0], CHUNK):
        rows = pl.ds(at, CHUNK)
        w = jnp.exp2(chunk_scores(kv, kpos, qpos, q_scr[...], at) - lse)
        dp = mm(kv[rows, HEAD_DIM:], u_scr[...], NT)
        ds = (w * (dp - delta)).astype(jnp.bfloat16)
        terms_ref[rows, HEAD_DIM:] = mm(w.astype(jnp.bfloat16), u_scr[...], NN).astype(jnp.bfloat16)
        terms_ref[rows, :HEAD_DIM] = (mm(ds, q_scr[...], NN) * FACTOR).astype(jnp.bfloat16)
        dq = mm(kv[rows, :HEAD_DIM].T, ds, NN)
        dq_scr[...] = dq if at == 0 else dq_scr[...] + dq
    n = own_ref.shape[0]
    for h in range(GROUPS):
        for g, ref in enumerate((own_ref, far_ref, core_ref, both_ref)):
            at = (4 * h + g) * n
            part = (dq_scr[:, at : at + n] * FACTOR).T
            ref[:, h * HEAD_DIM : (h + 1) * HEAD_DIM] = part.astype(ref.dtype)


def upstream_kernel(order, *refs):
    parts, w_hbm, out, w, sems = refs[:-4], *refs[-4:]
    rows, width = out.shape[0], parts[0].shape[1]
    copies = []
    for i in range(order.shape[0]):
        at = pl.multiple_of(order[i] * width, width)
        copies.append(pltpu.make_async_copy(w_hbm.at[:, pl.ds(at, width)], w.at[i], sems.at[i]))
        copies[-1].start()
    total, i = None, 0
    for part in parts:
        for at in range(0, part.shape[0], rows):
            copies[i].wait()
            term = mm(part[at : at + rows, :], w[i], NT)
            total = term if total is None else total + term
            i += 1
    out[...] = total.astype(out.dtype)


def upstream_of(parts, order, o_weight):
    width = parts[0].shape[1]
    cols = o_weight.shape[0]
    count = order.shape[0]
    rows = sum(p.shape[0] for p in parts) // count
    vmem = pl.BlockSpec(memory_space=pltpu.VMEM)
    return pl.pallas_call(
        upstream_kernel,
        out_shape=jax.ShapeDtypeStruct((rows, cols), jnp.bfloat16),
        in_specs=[pl.BlockSpec(memory_space=pltpu.SMEM)]
        + [vmem] * len(parts)
        + [pl.BlockSpec(memory_space=pltpu.HBM)],
        out_specs=vmem,
        scratch_shapes=[
            pltpu.VMEM((count, cols, width), jnp.bfloat16),
            pltpu.SemaphoreType.DMA((count,)),
        ],
        compiler_params=pltpu.CompilerParams(vmem_limit_bytes=VMEM_LIMIT),
        name="upstream",
    )(order, *parts, pltpu.with_memory_space_constraint(o_weight, pltpu.HBM))


def pack_kernel(k, v, out):
    rows = k.shape[0]
    for at in range(0, out.shape[0], rows):
        out[at : at + rows, :HEAD_DIM] = k[...]
        out[at : at + rows, HEAD_DIM:] = v[...]


def packed(key_states, value_states, copies):
    rows, width = key_states.shape
    vmem = pl.BlockSpec(memory_space=pltpu.VMEM)
    return pl.pallas_call(
        pack_kernel,
        out_shape=jax.ShapeDtypeStruct((copies * rows, 2 * width), key_states.dtype),
        in_specs=[vmem, vmem],
        out_specs=vmem,
        cost_estimate=pl.CostEstimate(flops=0, transcendentals=0, bytes_accessed=12 * key_states.size),
        name="pack",
    )(key_states, value_states)


def local(queries, key_states, value_states, out_grad, o_weight, span_order):
    rows = queries.shape[0]
    nz = lax.axis_size("z")
    nx = lax.axis_size("x")
    keys = nz * rows
    many = 4 * rows
    f32, bf16 = jnp.float32, jnp.bfloat16
    yh, z, c = lax.axis_index("yh"), lax.axis_index("z"), lax.axis_index("c")
    yl, x = lax.axis_index("yl"), lax.axis_index("x")

    both = packed(key_states, value_states, nz).reshape(nz, rows, 2 * HEAD_DIM)
    kv = lax.all_to_all(both, "z", 0, 0, tiled=True).reshape(keys, 2 * HEAD_DIM)

    pair = jnp.concatenate((out_grad, shift_by(out_grad, ("yl",), (1,))), axis=0)
    parts, sources = [], []
    for step in (0, 1, 3, 2):
        parts.append(shift_by(pair, ("x",), (step,)) if step else pair)
        near = (x - step) % nx
        sources += [yl * nx + near, (1 - yl) * nx + near]
    order = jnp.stack(sources).astype(jnp.int32)

    def shared(own):
        far = shift_by(own, ("yh",), (1,))
        return own, far, shift_by(own, ("c",), (1,)), shift_by(far, ("c",), (1,))

    def everyone(own):
        return (
            own,
            shift_by(own, ("yh",), (1,)),
            shift_by(own, ("c",), (1,)),
            shift_by(own, ("yh", "c"), (1, 1)),
        )

    spans = span_order.reshape(2, nz, 2, 2)
    offsets = jnp.arange(SPAN, dtype=jnp.int32)
    key_spans = lax.dynamic_slice(spans, (yh, 0, c, 0), (1, nz, 1, 2)).reshape(2 * nz, 1)
    kpos = (key_spans * SPAN + offsets[None, :]).reshape(keys, 1)
    groups = [(yh, c), (1 - yh, c), (yh, 1 - c), (1 - yh, 1 - c)]
    query_spans = jnp.concatenate(
        [lax.dynamic_slice(spans, (a, z, b, 0), (1, 1, 1, 2)).reshape(2, 1) for a, b in groups]
    )
    qpos = (query_spans * SPAN + offsets[None, :]).reshape(1, many)

    vmem = pl.BlockSpec(memory_space=pltpu.VMEM)
    wide = pltpu.VMEM((GROUPS * many, HEAD_DIM), bf16)
    params = pltpu.CompilerParams(vmem_limit_bytes=VMEM_LIMIT)

    held, pair, kpos, qpos = lax.optimization_barrier((queries, pair, kpos, qpos))
    q = shared(held)
    lse = pl.pallas_call(
        stats_kernel,
        out_shape=jax.ShapeDtypeStruct((1, GROUPS * many), f32),
        in_specs=[vmem] * 7,
        out_specs=vmem,
        scratch_shapes=[wide, pltpu.VMEM((keys, GROUPS * many), f32)],
        compiler_params=params,
        name="row_stats",
    )(kpos, qpos, *q, kv)

    upstream = upstream_of(parts, order, o_weight)
    far, core = shift_by(upstream, ("yh",), (1,)), shift_by(upstream, ("c",), (1,))
    narrow = pltpu.VMEM((GROUPS * many // 2, HEAD_DIM), bf16)
    near_delta = pl.pallas_call(
        near_delta_kernel,
        out_shape=jax.ShapeDtypeStruct((1, GROUPS * many // 2), f32),
        in_specs=[vmem] * 8,
        out_specs=vmem,
        scratch_shapes=[narrow, narrow],
        compiler_params=params,
        name="near_delta",
    )(kpos, qpos, q[0], q[2], upstream, core, kv, lse)
    far, near_delta = lax.optimization_barrier((far, near_delta))
    u = upstream, far, core, shift_by(far, ("c",), (1,))
    stats = pl.pallas_call(
        far_delta_kernel,
        out_shape=jax.ShapeDtypeStruct((2, GROUPS * many), f32),
        in_specs=[vmem] * 9,
        out_specs=vmem,
        scratch_shapes=[narrow, narrow],
        compiler_params=params,
        name="far_delta",
    )(kpos, qpos, q[1], q[3], u[1], u[3], kv, lse, near_delta)
    stats_parts = everyone(stats)

    shape = (rows, GROUPS * HEAD_DIM)
    own, far, core, across, terms = pl.pallas_call(
        grad_kernel,
        out_shape=(
            jax.ShapeDtypeStruct(shape, f32),
            jax.ShapeDtypeStruct(shape, f32),
            jax.ShapeDtypeStruct(shape, bf16),
            jax.ShapeDtypeStruct(shape, bf16),
            jax.ShapeDtypeStruct((keys, 2 * HEAD_DIM), bf16),
        ),
        in_specs=[vmem] * 15,
        out_specs=(vmem,) * 5,
        scratch_shapes=[wide, wide, pltpu.VMEM((HEAD_DIM, GROUPS * many), f32)],
        compiler_params=params,
        name="gradients",
    )(kpos, qpos, *q, *u, kv, *stats_parts)

    summed = lax.all_to_all(terms.reshape(nz, rows, 2 * HEAD_DIM), "z", 0, 0, tiled=True)
    summed = jnp.sum(summed.astype(f32), axis=0)
    own = own + shift_by(core, ("c",), (1,)).astype(f32)
    far = far + shift_by(across, ("c",), (1,)).astype(f32)
    query_grad = own + shift_by(far.astype(bf16), ("yh",), (1,)).astype(f32)
    return query_grad, summed[:, :HEAD_DIM], summed[:, HEAD_DIM:]


def solution(mesh):
    finer = Mesh(mesh.devices.reshape(2, 8, 2, 2, 4), CP + VOCAB)
    return jax.shard_map(
        local,
        mesh=finer,
        in_specs=(P(CP, VOCAB), P(CP, VOCAB), P(CP, VOCAB), P(CP, VOCAB), P(VOCAB, None), P()),
        out_specs=(P(CP, VOCAB), P(CP, VOCAB), P(CP, VOCAB)),
        check_vma=False,
    )
```

```python
import math

import jax
import jax.numpy as jnp
from jax import lax
from jax.experimental import pallas as pl
from jax.experimental.pallas import tpu as pltpu
from jax.sharding import Mesh
from jax.sharding import PartitionSpec as P

HEADS = 32
KV_HEADS = 8
HEAD_DIM = 128
GROUPS = HEADS // KV_HEADS
SPAN = 64
CP = ("yh", "z", "c")
VOCAB = ("yl", "x")
FACTOR = HEAD_DIM**-0.5
SCALE2 = FACTOR * math.log2(math.e)
MASKED = -1e30
CHUNK = 512
GRAD_CHUNK = 1024
VMEM_LIMIT = 40 * 1024 * 1024
NT = (((1,), (1,)), ((), ()))
NN = (((1,), (0,)), ((), ()))


def mm(a, b, dims):
    return lax.dot_general(a, b, dims, preferred_element_type=jnp.float32)


def shift_by(value, axes, steps):
    sizes = [lax.axis_size(a) for a in axes]
    total = math.prod(sizes)
    pairs = []
    for src in range(total):
        rest, at = src, []
        for n in reversed(sizes):
            at.insert(0, rest % n)
            rest //= n
        dst = 0
        for n, i, s in zip(sizes, at, steps):
            dst = dst * n + (i + s) % n
        pairs.append((src, dst))
    return lax.ppermute(value, axes, pairs)


def by_heads(refs):
    return jnp.concatenate(
        [r[:, h * HEAD_DIM : (h + 1) * HEAD_DIM] for h in range(GROUPS) for r in refs], axis=0
    )


def chunk_scores(k, kpos, qpos, q, at, size=CHUNK):
    rows = pl.ds(at, size)
    bias = jnp.where(kpos[rows, :] <= qpos[...], 0.0, MASKED)
    bias = jnp.concatenate([bias] * GROUPS, axis=1)
    return mm(k[rows, :HEAD_DIM], q, NT) * SCALE2 + bias


def stats_kernel(kpos, qpos, q0, q1, q2, q3, kv, lse_ref, q_scr, s_scr):
    q_scr[...] = by_heads((q0, q1, q2, q3))
    keys = kv.shape[0]
    peak = jnp.full((1, q_scr.shape[0]), MASKED, jnp.float32)
    for at in range(0, keys, CHUNK):
        s = chunk_scores(kv, kpos, qpos, q_scr[...], at)
        s_scr[pl.ds(at, CHUNK), :] = s
        peak = jnp.maximum(peak, jnp.max(s, axis=0, keepdims=True))
    total = jnp.zeros_like(peak)
    for at in range(0, keys, CHUNK):
        total = total + jnp.sum(jnp.exp2(s_scr[pl.ds(at, CHUNK), :] - peak), axis=0, keepdims=True)
    lse_ref[...] = peak + jnp.log2(total)


def aligned(own, far, core, both):
    n = own.shape[1] // (4 * GROUPS)

    def pick(a, order):
        return jnp.concatenate(
            [a[:, (4 * h + g) * n : (4 * h + g + 1) * n] for h in range(GROUPS) for g in order],
            axis=1,
        )

    return own, pick(far, (1, 0, 3, 2)), pick(core, (2, 3, 0, 1)), pick(both, (3, 2, 1, 0))


def half_delta(kpos, qpos, q_refs, u_refs, kv, lse, q_scr, u_scr, groups):
    n = qpos.shape[1] // 4
    q_scr[...] = by_heads(q_refs)
    u_scr[...] = by_heads(u_refs)
    places = jnp.concatenate([qpos[:, g * n : (g + 1) * n] for g in groups], axis=1)
    lse = jnp.concatenate(
        [lse[:, (4 * h + g) * n : (4 * h + g + 1) * n] for h in range(GROUPS) for g in groups],
        axis=1,
    )
    total = jnp.zeros_like(lse)
    for at in range(0, kv.shape[0], CHUNK):
        w = jnp.exp2(chunk_scores(kv, kpos, places, q_scr[...], at) - lse)
        dp = mm(kv[pl.ds(at, CHUNK), HEAD_DIM:], u_scr[...], NT)
        total = total + jnp.sum(w * dp, axis=0, keepdims=True)
    return total


def near_delta_kernel(kpos, qpos, q0, q2, u0, u2, kv, lse, out, q_scr, u_scr):
    out[...] = half_delta(kpos, qpos, (q0, q2), (u0, u2), kv, lse, q_scr, u_scr, (0, 2))


def far_delta_kernel(kpos, qpos, q1, q3, u1, u3, kv, lse, near, stats_ref, q_scr, u_scr):
    far = half_delta(kpos, qpos, (q1, q3), (u1, u3), kv, lse, q_scr, u_scr, (1, 3))
    n = qpos.shape[1] // 4
    stats_ref[0:1, :] = lse[...]
    for h in range(GROUPS):
        for g in range(4):
            half = far[:, :] if g % 2 else near[...]
            at = 2 * h + g // 2
            stats_ref[1:2, (4 * h + g) * n : (4 * h + g + 1) * n] = half[:, at * n : (at + 1) * n]


def grad_kernel(
    kpos, qpos, q0, q1, q2, q3, u0, u1, u2, u3, kv, s0, s1, s2, s3,
    own_ref, far_ref, core_ref, both_ref, terms_ref, q_scr, u_scr, dq_scr,
):
    q_scr[...] = by_heads((q0, q1, q2, q3))
    u_scr[...] = by_heads((u0, u1, u2, u3))
    parts = aligned(s0[...], s1[...], s2[...], s3[...])
    peak = jnp.maximum(
        jnp.maximum(parts[0][:1], parts[1][:1]), jnp.maximum(parts[2][:1], parts[3][:1])
    )
    shares = [jnp.exp2(p[:1] - peak) for p in parts]
    whole_share = sum(shares)
    lse = peak + jnp.log2(whole_share)
    delta = sum(p[1:] * share for p, share in zip(parts, shares)) / whole_share

    for at in range(0, kv.shape[0], GRAD_CHUNK):
        rows = pl.ds(at, GRAD_CHUNK)
        w = jnp.exp2(chunk_scores(kv, kpos, qpos, q_scr[...], at, GRAD_CHUNK) - lse)
        dp = mm(kv[rows, HEAD_DIM:], u_scr[...], NT)
        ds = (w * (dp - delta)).astype(jnp.bfloat16)
        terms_ref[rows, HEAD_DIM:] = mm(w.astype(jnp.bfloat16), u_scr[...], NN).astype(jnp.bfloat16)
        terms_ref[rows, :HEAD_DIM] = (mm(ds, q_scr[...], NN) * FACTOR).astype(jnp.bfloat16)
        dq = mm(kv[rows, :HEAD_DIM].T, ds, NN)
        dq_scr[...] = dq if at == 0 else dq_scr[...] + dq
    n = own_ref.shape[0]
    for h in range(GROUPS):
        for g, ref in enumerate((own_ref, far_ref, core_ref, both_ref)):
            at = (4 * h + g) * n
            part = (dq_scr[:, at : at + n] * FACTOR).T
            ref[:, h * HEAD_DIM : (h + 1) * HEAD_DIM] = part.astype(ref.dtype)


def upstream_kernel(order, *refs):
    parts, w_hbm, out, w, sems = refs[:-4], *refs[-4:]
    rows, width = out.shape[0], parts[0].shape[1]
    copies = []
    for i in range(order.shape[0]):
        at = pl.multiple_of(order[i] * width, width)
        copies.append(pltpu.make_async_copy(w_hbm.at[:, pl.ds(at, width)], w.at[i], sems.at[i]))
        copies[-1].start()
    total, i = None, 0
    for part in parts:
        for at in range(0, part.shape[0], rows):
            copies[i].wait()
            term = mm(part[at : at + rows, :], w[i], NT)
            total = term if total is None else total + term
            i += 1
    out[...] = total.astype(out.dtype)


def upstream_of(parts, order, o_weight):
    width = parts[0].shape[1]
    cols = o_weight.shape[0]
    count = order.shape[0]
    rows = sum(p.shape[0] for p in parts) // count
    vmem = pl.BlockSpec(memory_space=pltpu.VMEM)
    return pl.pallas_call(
        upstream_kernel,
        out_shape=jax.ShapeDtypeStruct((rows, cols), jnp.bfloat16),
        in_specs=[pl.BlockSpec(memory_space=pltpu.SMEM)]
        + [vmem] * len(parts)
        + [pl.BlockSpec(memory_space=pltpu.HBM)],
        out_specs=vmem,
        scratch_shapes=[
            pltpu.VMEM((count, cols, width), jnp.bfloat16),
            pltpu.SemaphoreType.DMA((count,)),
        ],
        compiler_params=pltpu.CompilerParams(vmem_limit_bytes=VMEM_LIMIT),
        name="upstream",
    )(order, *parts, pltpu.with_memory_space_constraint(o_weight, pltpu.HBM))


def pack_kernel(k, v, out):
    rows = k.shape[0]
    for at in range(0, out.shape[0], rows):
        out[at : at + rows, :HEAD_DIM] = k[...]
        out[at : at + rows, HEAD_DIM:] = v[...]


def packed(key_states, value_states, copies):
    rows, width = key_states.shape
    vmem = pl.BlockSpec(memory_space=pltpu.VMEM)
    return pl.pallas_call(
        pack_kernel,
        out_shape=jax.ShapeDtypeStruct((copies * rows, 2 * width), key_states.dtype),
        in_specs=[vmem, vmem],
        out_specs=vmem,
        cost_estimate=pl.CostEstimate(flops=0, transcendentals=0, bytes_accessed=12 * key_states.size),
        name="pack",
    )(key_states, value_states)


def local(queries, key_states, value_states, out_grad, o_weight, span_order):
    rows = queries.shape[0]
    nz = lax.axis_size("z")
    nx = lax.axis_size("x")
    keys = nz * rows
    many = 4 * rows
    f32, bf16 = jnp.float32, jnp.bfloat16
    yh, z, c = lax.axis_index("yh"), lax.axis_index("z"), lax.axis_index("c")
    yl, x = lax.axis_index("yl"), lax.axis_index("x")

    both = packed(key_states, value_states, nz).reshape(nz, rows, 2 * HEAD_DIM)
    kv = lax.all_to_all(both, "z", 0, 0, tiled=True).reshape(keys, 2 * HEAD_DIM)

    pair = jnp.concatenate((out_grad, shift_by(out_grad, ("yl",), (1,))), axis=0)
    parts, sources = [], []
    for step in (0, 1, 3, 2):
        parts.append(shift_by(pair, ("x",), (step,)) if step else pair)
        near = (x - step) % nx
        sources += [yl * nx + near, (1 - yl) * nx + near]
    order = jnp.stack(sources).astype(jnp.int32)

    def shared(own):
        far = shift_by(own, ("yh",), (1,))
        return own, far, shift_by(own, ("c",), (1,)), shift_by(far, ("c",), (1,))

    def everyone(own):
        return (
            own,
            shift_by(own, ("yh",), (1,)),
            shift_by(own, ("c",), (1,)),
            shift_by(own, ("yh", "c"), (1, 1)),
        )

    spans = span_order.reshape(2, nz, 2, 2)
    offsets = jnp.arange(SPAN, dtype=jnp.int32)
    key_spans = lax.dynamic_slice(spans, (yh, 0, c, 0), (1, nz, 1, 2)).reshape(2 * nz, 1)
    kpos = (key_spans * SPAN + offsets[None, :]).reshape(keys, 1)
    groups = [(yh, c), (1 - yh, c), (yh, 1 - c), (1 - yh, 1 - c)]
    query_spans = jnp.concatenate(
        [lax.dynamic_slice(spans, (a, z, b, 0), (1, 1, 1, 2)).reshape(2, 1) for a, b in groups]
    )
    qpos = (query_spans * SPAN + offsets[None, :]).reshape(1, many)

    vmem = pl.BlockSpec(memory_space=pltpu.VMEM)
    wide = pltpu.VMEM((GROUPS * many, HEAD_DIM), bf16)
    params = pltpu.CompilerParams(vmem_limit_bytes=VMEM_LIMIT)

    held, pair, kpos, qpos = lax.optimization_barrier((queries, pair, kpos, qpos))
    q = shared(held)
    lse = pl.pallas_call(
        stats_kernel,
        out_shape=jax.ShapeDtypeStruct((1, GROUPS * many), f32),
        in_specs=[vmem] * 7,
        out_specs=vmem,
        scratch_shapes=[wide, pltpu.VMEM((keys, GROUPS * many), f32)],
        compiler_params=params,
        name="row_stats",
    )(kpos, qpos, *q, kv)

    upstream = upstream_of(parts, order, o_weight)
    far, core = shift_by(upstream, ("yh",), (1,)), shift_by(upstream, ("c",), (1,))
    narrow = pltpu.VMEM((GROUPS * many // 2, HEAD_DIM), bf16)
    near_delta = pl.pallas_call(
        near_delta_kernel,
        out_shape=jax.ShapeDtypeStruct((1, GROUPS * many // 2), f32),
        in_specs=[vmem] * 8,
        out_specs=vmem,
        scratch_shapes=[narrow, narrow],
        compiler_params=params,
        name="near_delta",
    )(kpos, qpos, q[0], q[2], upstream, core, kv, lse)
    far, near_delta = lax.optimization_barrier((far, near_delta))
    u = upstream, far, core, shift_by(far, ("c",), (1,))
    stats = pl.pallas_call(
        far_delta_kernel,
        out_shape=jax.ShapeDtypeStruct((2, GROUPS * many), f32),
        in_specs=[vmem] * 9,
        out_specs=vmem,
        scratch_shapes=[narrow, narrow],
        compiler_params=params,
        name="far_delta",
    )(kpos, qpos, q[1], q[3], u[1], u[3], kv, lse, near_delta)
    stats_parts = everyone(stats)

    shape = (rows, GROUPS * HEAD_DIM)
    own, far, core, across, terms = pl.pallas_call(
        grad_kernel,
        out_shape=(
            jax.ShapeDtypeStruct(shape, f32),
            jax.ShapeDtypeStruct(shape, f32),
            jax.ShapeDtypeStruct(shape, bf16),
            jax.ShapeDtypeStruct(shape, bf16),
            jax.ShapeDtypeStruct((keys, 2 * HEAD_DIM), bf16),
        ),
        in_specs=[vmem] * 15,
        out_specs=(vmem,) * 5,
        scratch_shapes=[wide, wide, pltpu.VMEM((HEAD_DIM, GROUPS * many), f32)],
        compiler_params=params,
        name="gradients",
    )(kpos, qpos, *q, *u, kv, *stats_parts)

    summed = lax.all_to_all(terms.reshape(nz, rows, 2 * HEAD_DIM), "z", 0, 0, tiled=True)
    summed = jnp.sum(summed.astype(f32), axis=0)
    own = own + shift_by(core, ("c",), (1,)).astype(f32)
    far = far + shift_by(across, ("c",), (1,)).astype(f32)
    query_grad = own + shift_by(far.astype(bf16), ("yh",), (1,)).astype(f32)
    return query_grad, summed[:, :HEAD_DIM], summed[:, HEAD_DIM:]


def solution(mesh):
    finer = Mesh(mesh.devices.reshape(2, 8, 2, 2, 4), CP + VOCAB)
    return jax.shard_map(
        local,
        mesh=finer,
        in_specs=(P(CP, VOCAB), P(CP, VOCAB), P(CP, VOCAB), P(CP, VOCAB), P(VOCAB, None), P()),
        out_specs=(P(CP, VOCAB), P(CP, VOCAB), P(CP, VOCAB)),
        check_vma=False,
    )
```
